128 devices in a mesh: src: 8 (over y, z_lo), rcv: 16 (over x, z_hi, core).
Axes of the slice: x: 4, y: 4, z: 4 (z_hi: 2, z_lo: 2; z = z_hi * 2 + z_lo), core: 2. Of those that a mesh axis runs over, the one named last changes fastest.
Arguments:
- traces: float32 [512, 512, 1024], P('src', 'rcv'), may hold values from -6 to 6
- freq_index: int32 [256], replicated, may hold values from 1 to 511, as said below
- primaries: float32 [256, 2, 512, 512], P(('src', 'rcv')), may hold values from -0.1875 to 0.1875
Outputs:
- residual: float32 [256, 2, 512, 512], P(('src', 'rcv'))
- residual_next: float32 [256, 2, 512, 512], P(('src', 'rcv'))
The draws below stay inside these ranges and needn't reach their ends.
Inputs may be any that keep to these rules, and one draw needn't show every extreme that they name: `freq_index`: sorted ascending; repeats possible; the first is 1 and the last is 511.
All inputs are finite; a program needn't handle non-finite values.
Results may differ from the reference program's by a relative error of at most 0.00012.
Values sent between devices are 32-bit elements; how exact they have to be, the bound alone decides.
A program may use at most 128 MiB of HBM per device.

```python
import math
import jax
import jax.numpy as jnp
from jax import lax

NS = 512
NR = 512
NT = 1024
NF = 256
N_SRC = 8


def draw_freq_index(key, part):
    values = jax.random.randint(jax.random.fold_in(key, 17), (NF,), 1, NT // 2)
    values = values.at[0].set(1).at[NF - 1].set(NT // 2 - 1)
    return jnp.sort(values).astype(jnp.int32)


def levels(own_key, extent, split, low, top_value):
    loudness = 1.0
    for position, blocks in split:
        draws = jax.random.uniform(jax.random.fold_in(jax.random.fold_in(own_key, 6), position), (blocks,), jnp.float32, low / len(split), top_value / len(split))
        loudness = loudness * jnp.repeat(jnp.exp(draws), extent[position] // blocks).reshape((-1,) + (1,) * (len(extent) - 1 - position))
    return loudness


def gaussian(own_key, shape, spread, most, pieces=(), kind=jnp.bfloat16):
    entries = jax.random.normal(own_key, shape, jnp.float32) * spread
    if len(pieces) > 0:
        entries = levels(own_key, shape, pieces, -0.22, 0.18) * entries
    return jnp.clip(entries, min=-most, max=most).astype(kind)


def setup_inputs(seed: int = 0) -> dict:
    key_of = jax.random.split(jax.random.key(seed), 4)
    traces = gaussian(key_of[0], (NS, NR, NT), 1.0, 6.0, ((0, 8), (1, 16)), jnp.float32)
    freq_index = draw_freq_index(jax.random.fold_in(key_of[3], 71), 0)
    primaries = gaussian(key_of[2], (NF, 2, NS, NR), (2 * NS) ** -0.5, 0.1875, ((0, 128),), jnp.float32)
    return dict(traces=traces, freq_index=freq_index, primaries=primaries)


def freq_table(freq_index, samples):
    times = jnp.arange(samples, dtype=jnp.int32)
    phase = freq_index[:, None] * times[None, :] % samples
    angle = phase.astype(jnp.float32) * (2.0 * math.pi / samples)
    return jnp.stack([jnp.cos(angle), -jnp.sin(angle)], axis=1) / math.sqrt(samples)

def matrix_product(left, right):
    return jnp.einsum('fij,fjk->fik', left, right, precision=lax.Precision.HIGHEST)

def complex_product(left_re, left_im, right_re, right_im, adjoint):
    if adjoint:
        right_re = jnp.swapaxes(right_re, 1, 2)
        right_im = -jnp.swapaxes(right_im, 1, 2)
    real_part = matrix_product(left_re, right_re) - matrix_product(left_im, right_im)
    imag_part = matrix_product(left_re, right_im) + matrix_product(left_im, right_re)
    return (real_part, imag_part)

def solve_step(spectrum, primaries, weights):
    data_re = 0.5 * (spectrum[:, 0] + jnp.swapaxes(spectrum[:, 0], 1, 2))
    data_im = 0.5 * (spectrum[:, 1] + jnp.swapaxes(spectrum[:, 1], 1, 2))
    model_re, model_im = complex_product(primaries[:, 0], primaries[:, 1], data_re, data_im, False)
    resid_re = data_re - model_re
    resid_im = data_im - model_im
    grad_re, grad_im = complex_product(resid_re, resid_im, data_re, data_im, True)
    pred_re, pred_im = complex_product(grad_re, grad_im, data_re, data_im, False)
    scaled = weights[:, None, None]
    numer = jnp.sum(scaled * (resid_re * pred_re + resid_im * pred_im))
    denom = jnp.sum(scaled * (pred_re * pred_re + pred_im * pred_im))
    return (jnp.stack([resid_re, resid_im], 1), jnp.stack([pred_re, pred_im], 1), numer, denom)

def reference(traces, freq_index, primaries):
    table = freq_table(freq_index, NT)
    blocks = traces.reshape(N_SRC, NS // N_SRC, NR, NT)

    def transform(block):
        return jnp.einsum('kct,srt->kcsr', table, block, precision=lax.Precision.HIGHEST)
    spectrum = lax.map(transform, blocks)
    spectrum = jnp.transpose(spectrum, (1, 2, 0, 3, 4)).reshape(NF, 2, NS, NR)
    weights = freq_index.astype(jnp.float32) / (NT // 2)

    def per_freq(items):
        return solve_step(items[0], items[1], items[2])
    resid, pred, numer, denom = lax.map(per_freq, (spectrum[:, None], primaries[:, None], weights[:, None]))
    resid = resid.reshape(NF, 2, NS, NR)
    pred = pred.reshape(NF, 2, NS, NR)
    step_size = jnp.sum(numer) / jnp.sum(denom)
    return (resid, resid - step_size * pred)
```

```python
import math
import random

import jax
import jax.numpy as jnp
from jax import lax
from jax.experimental import pallas as pl
from jax.experimental.pallas import tpu as pltpu
from jax.sharding import PartitionSpec as P

MESH = pl.DeviceIdType.MESH
F32, BF16 = jnp.float32, jnp.bfloat16
NN = (((1,), (0,)), ((), ()))
NT = (((1,), (1,)), ((), ()))
N = 512
DEVICES = 128


def displacements():
    every = [(x, y, z, c) for x in range(4) for y in range(4) for z in range(4) for c in range(2)]
    every = every[1:]
    random.Random(0).shuffle(every)
    return every


def halves(x):
    high = x.astype(BF16)
    return high, (x - high.astype(F32)).astype(BF16)


def dot3(left, right, dims=NN):
    def one(a, b):
        return lax.dot_general(a, b, dims, preferred_element_type=F32)

    return one(left[0], right[0]) + (one(left[0], right[1]) + one(left[1], right[0]))


def cos_sin(steps):
    quarter = (steps + 128) >> 8
    angle = (steps - quarter * 256).astype(F32) * (2.0 * math.pi / 1024)
    square = angle * angle
    cos = 1.0 / 40320 - square * (1.0 / 3628800)
    for term in (-1.0 / 720, 1.0 / 24, -0.5, 1.0):
        cos = term + square * cos
    sin = -1.0 / 5040 + square * (1.0 / 362880)
    for term in (1.0 / 120, -1.0 / 6, 1.0):
        sin = term + square * sin
    sin = angle * sin
    quarter = quarter & 3
    odd = (quarter & 1) == 1
    cos, sin = jnp.where(odd, sin, cos), jnp.where(odd, cos, sin)
    cos = jnp.where((quarter == 1) | (quarter == 2), -cos, cos)
    sin = jnp.where(quarter >= 2, -sin, sin)
    return cos, sin


def kernel(
    traces_ref, freq_ref, weight_ref, prim_ref,
    resid_out, pred_out, step_out,
    raw, xh, xl, th, tl, sbuf, rbuf, prim, ah, al, whole, dh, dl, rh, rl, hh, hl, resid, pred, stat, slots,
    raw_sem, prim_sem, send_sem, recv_sem, own_sem, out_sem, stat_send, stat_recv,
):
    src, rcv = lax.axis_index("src"), lax.axis_index("rcv")
    me = src * 16 + rcv
    xs = [(rcv // 4 + d) % 4 for d in range(4)]
    ys = [(src // 2 + d) % 4 for d in range(4)]
    zs = [((rcv // 2) % 2 * 2 + src % 2 + d) % 4 for d in range(4)]
    cores = [(rcv + d) % 2 for d in range(2)]
    src_of = [[ys[y] * 2 + zs[z] % 2 for z in range(4)] for y in range(4)]
    rcv_of = [[[xs[x] * 4 + zs[z] // 2 * 2 + cores[c] for c in range(2)] for z in range(4)] for x in range(4)]
    order = displacements()

    def target(disp):
        x, y, z, c = disp
        return src_of[y][z], rcv_of[x][z][c]

    def load(b, g):
        return pltpu.make_async_copy(traces_ref.at[g, pl.ds(b * 4, 4)], raw.at[b, :, g], raw_sem.at[b])

    for b in range(4):
        for g in range(4):
            load(b, g).start()
    prim_copy = pltpu.make_async_copy(prim_ref, prim, prim_sem)
    prim_copy.start()

    barrier = pltpu.get_barrier_semaphore()
    for disp in order:
        pl.semaphore_signal(barrier, inc=1, device_id=target(disp), device_id_type=MESH)

    lane = lax.broadcasted_iota(jnp.int32, (128, 128), 1)
    for j in range(2):
        freq = freq_ref[pl.ds(j * 128, 128), :]
        cos, sin = cos_sin((freq * lane) & 1023)
        cos, sin = cos * 0.03125, sin * 0.03125
        turn_cos, turn_sin = cos_sin((freq * 128) & 1023)
        sign = 1.0 - 2.0 * (freq & 1).astype(F32)
        for a in range(4):
            if a:
                cos, sin = cos * turn_cos - sin * turn_sin, sin * turn_cos + cos * turn_sin
            for c, part in enumerate((cos, -sin)):
                for k, value in ((a, part), (a + 4, part * sign)):
                    high, low = halves(value)
                    th[j, c * 128 : c * 128 + 128, k * 128 : k * 128 + 128] = high
                    tl[j, c * 128 : c * 128 + 128, k * 128 : k * 128 + 128] = low

    def transform(j, b):
        rows = pl.ds(pl.multiple_of(b * 512, 512), 512)
        out = dot3((th[j], tl[j]), (xh[rows, :], xl[rows, :]), NT)
        for c in range(2):
            for d in range(0, 128, 8):
                for i in range(4):
                    start = j * DEVICES * 32 + d * 32 + c * 16 + b * 4 + i
                    sbuf[pl.ds(start, 8, stride=32), :] = out[
                        c * 128 + d : c * 128 + d + 8, i * 128 : i * 128 + 128
                    ]

    def piece(j, index):
        return pl.ds(pl.multiple_of((j * DEVICES + index) * 32, 32), 32)

    def remote(j, disp):
        to_src, to_rcv = target(disp)
        return pltpu.make_async_remote_copy(
            src_ref=sbuf.at[piece(j, to_src * 16 + to_rcv)],
            dst_ref=rbuf.at[piece(j, me)],
            send_sem=send_sem.at[j],
            recv_sem=recv_sem.at[j],
            device_id=(to_src, to_rcv),
            device_id_type=MESH,
        )

    def own(j):
        return pltpu.make_async_copy(sbuf.at[piece(j, me)], rbuf.at[piece(j, me)], own_sem.at[j])

    @pl.loop(0, 4)
    def _(b):
        for g in range(4):
            load(b, g).wait()
        high, low = halves(raw[b].reshape(512, 1024))
        rows = pl.ds(pl.multiple_of(b * 512, 512), 512)
        xh[rows, :] = high
        xl[rows, :] = low
        transform(0, b)

    pl.semaphore_wait(barrier, DEVICES - 1)
    own(0).start()
    for disp in order:
        remote(0, disp).start()

    @pl.loop(0, 4)
    def _(b):
        transform(1, b)

    own(1).start()
    for disp in order:
        remote(1, disp).start()

    prim_copy.wait()

    wide = lax.broadcasted_iota(jnp.int32, (32, 128), 1)
    odd, upper = (wide // 32) % 2 == 1, wide >= 64
    lanes = lax.broadcasted_iota(jnp.int32, (1, 128), 1)
    total = jnp.zeros((1, 128), F32)

    def put(high_ref, low_ref, index, value):
        high, low = halves(value)
        high_ref[index] = high
        low_ref[index] = low

    def pair(high_ref, low_ref, index):
        return high_ref[index], low_ref[index]

    for j in range(2):
        put(ah, al, 0, prim[j, 0] + prim[j, 1])
        put(ah, al, 1, prim[j, 0])
        put(ah, al, 2, prim[j, 1])

        arrived = pltpu.make_async_remote_copy(
            src_ref=sbuf.at[pl.ds(j * DEVICES * 32, 127 * 32)],
            dst_ref=rbuf.at[pl.ds(j * DEVICES * 32, 127 * 32)],
            send_sem=send_sem.at[j],
            recv_sem=recv_sem.at[j],
            device_id=target(order[0]),
            device_id_type=MESH,
        )
        own(j).wait()
        arrived.wait_recv()

        @pl.loop(0, 8)
        def _(s):
            for x in range(4):
                v = [rbuf[piece(j, s * 16 + x * 4 + q), :] for q in range(4)]
                for m in (0, 2):
                    a, b = v[m], v[m + 1]
                    v[m] = jnp.where(odd, pltpu.roll(b, 32, 1), a)
                    v[m + 1] = jnp.where(odd, b, pltpu.roll(a, 96, 1))
                for m in (0, 1):
                    a, b = v[m], v[m + 2]
                    v[m] = jnp.where(upper, pltpu.roll(b, 64, 1), a)
                    v[m + 2] = jnp.where(upper, b, pltpu.roll(a, 64, 1))
                for g in range(4):
                    rows = pl.ds(pl.multiple_of(s * 64 + g * 16, 16), 16)
                    whole[0, rows, x * 128 : x * 128 + 128] = v[g][:16]
                    whole[1, rows, x * 128 : x * 128 + 128] = v[g][16:]

        for p in range(4):
            for q in range(p, 4):
                a, b = slice(p * 128, p * 128 + 128), slice(q * 128, q * 128 + 128)
                parts = []
                for c in range(2):
                    value = 0.5 * (whole[c, a, b] + whole[c, b, a].T)
                    whole[c, a, b] = value
                    parts.append((value, value.T if p != q else None))
                for where_, (re, im) in (((a, b), (parts[0][0], parts[1][0])), ((b, a), (parts[0][1], parts[1][1]))):
                    if re is None:
                        continue
                    if where_ == (b, a) and p != q:
                        whole[0, b, a] = re
                        whole[1, b, a] = im
                    for index, value in enumerate((re, im - re, re + im, im)):
                        high, low = halves(value)
                        dh[index, where_[0], where_[1]] = high
                        dl[index, where_[0], where_[1]] = low

        d_re, d_dif, d_sum, d_im = (pair(dh, dl, i) for i in range(4))
        first = dot3(pair(ah, al, 0), d_re)
        second = dot3(pair(ah, al, 1), d_dif)
        third = dot3(pair(ah, al, 2), d_sum)
        re = whole[0] - (first - third)
        im = whole[1] - (first + second)
        resid[j, 0] = re
        resid[j, 1] = im
        put(rh, rl, 0, re + im)
        put(rh, rl, 1, re)
        put(rh, rl, 2, im)
        cross = -dot3(d_sum, d_dif)
        flipped = cross.T
        square = dot3(d_im, d_im)
        h_re = 0.5 * (cross + flipped) + 2.0 * square
        h_im = 0.5 * (flipped - cross)
        put(hh, hl, 0, h_re)
        put(hh, hl, 1, h_im - h_re)
        put(hh, hl, 2, h_im + h_re)
        first = dot3(pair(rh, rl, 0), pair(hh, hl, 0))
        second = dot3(pair(rh, rl, 1), pair(hh, hl, 1))
        third = dot3(pair(rh, rl, 2), pair(hh, hl, 2))
        re = first - third
        im = first + second
        pred[j, 0] = re
        pred[j, 1] = im
        numer = jnp.sum(resid[j, 0] * re + resid[j, 1] * im, axis=0, keepdims=True)
        denom = jnp.sum(re * re + im * im, axis=0, keepdims=True)
        fold = []
        for value in (numer, denom):
            value = value[:, :128] + value[:, 128:256] + value[:, 256:384] + value[:, 384:]
            fold.append(value + pltpu.roll(value, 64, 1))
        total += weight_ref[j : j + 1, :] * jnp.where(lanes < 64, fold[0], fold[1])
        pltpu.make_async_copy(resid.at[j], resid_out.at[j], out_sem.at[j, 0]).start()
        pltpu.make_async_copy(pred.at[j], pred_out.at[j], out_sem.at[j, 1]).start()
        arrived.wait_send()

    stat[0] = total
    slots[me] = total

    def share(disp):
        return pltpu.make_async_remote_copy(
            src_ref=stat.at[0],
            dst_ref=slots.at[me],
            send_sem=stat_send,
            recv_sem=stat_recv,
            device_id=target(disp),
            device_id_type=MESH,
        )

    for disp in order:
        share(disp).start()
    done = pltpu.make_async_remote_copy(
        src_ref=slots.at[pl.ds(0, 127)],
        dst_ref=slots.at[pl.ds(0, 127)],
        send_sem=stat_send,
        recv_sem=stat_recv,
        device_id=target(order[0]),
        device_id_type=MESH,
    )
    done.wait_recv()
    every = jnp.sum(slots[...], axis=0)
    numer = jnp.sum(jnp.where(lanes < 64, every, 0.0), axis=1, keepdims=True)
    denom = jnp.sum(jnp.where(lanes < 64, 0.0, every), axis=1, keepdims=True)
    step_out[...] = jnp.broadcast_to(numer / denom, (8, 128))
    done.wait_send()
    for j in range(2):
        pltpu.make_async_copy(resid.at[j], resid_out.at[j], out_sem.at[j, 0]).wait()
        pltpu.make_async_copy(pred.at[j], pred_out.at[j], out_sem.at[j, 1]).wait()


def on_device(traces, freq_index, primaries):
    me = lax.axis_index("src") * 16 + lax.axis_index("rcv")
    samples = traces.shape[2]
    freq = jnp.broadcast_to(freq_index.reshape(DEVICES, 2).T.reshape(256, 1), (256, 128))
    weight = lax.dynamic_slice_in_dim(freq_index, me * 2, 2).astype(F32) / (samples // 2)
    weight = jnp.broadcast_to(weight[:, None], (2, 128))
    anywhere, vmem = pl.BlockSpec(memory_space=pl.ANY), pl.BlockSpec(memory_space=pltpu.VMEM)
    big = jax.ShapeDtypeStruct((2, 2, N, N), F32)
    dma = pltpu.SemaphoreType.DMA
    resid, pred, step = pl.pallas_call(
        kernel,
        out_shape=(big, big, jax.ShapeDtypeStruct((8, 128), F32)),
        in_specs=[anywhere, vmem, vmem, anywhere],
        out_specs=(anywhere, anywhere, vmem),
        scratch_shapes=[
            pltpu.VMEM((4, 4, 4, 32, 1024), F32),
            pltpu.VMEM((2048, 1024), BF16),
            pltpu.VMEM((2048, 1024), BF16),
            pltpu.VMEM((2, 256, 1024), BF16),
            pltpu.VMEM((2, 256, 1024), BF16),
            pltpu.VMEM((2 * DEVICES * 32, 128), F32),
            pltpu.VMEM((2 * DEVICES * 32, 128), F32),
            pltpu.VMEM((2, 2, N, N), F32),
            pltpu.VMEM((3, N, N), BF16),
            pltpu.VMEM((3, N, N), BF16),
            pltpu.VMEM((2, N, N), F32),
            pltpu.VMEM((4, N, N), BF16),
            pltpu.VMEM((4, N, N), BF16),
            pltpu.VMEM((3, N, N), BF16),
            pltpu.VMEM((3, N, N), BF16),
            pltpu.VMEM((3, N, N), BF16),
            pltpu.VMEM((3, N, N), BF16),
            pltpu.VMEM((2, 2, N, N), F32),
            pltpu.VMEM((2, 2, N, N), F32),
            pltpu.VMEM((1, 1, 128), F32),
            pltpu.VMEM((DEVICES, 1, 128), F32),
            dma((4,)), dma, dma((2,)), dma((2,)), dma((2,)), dma((2, 2)), dma, dma,
        ],
        compiler_params=pltpu.CompilerParams(
            collective_id=0, has_side_effects=True, vmem_limit_bytes=64 * 2**20 - 65536
        ),
    )(traces.reshape(4, 16, 32, samples), freq, weight, primaries)
    return (resid, resid - step[0, 0] * pred)


def solution(mesh):
    spec = P(("src", "rcv"), None, None, None)
    return jax.shard_map(
        on_device, mesh=mesh, in_specs=(P("src", "rcv", None), P(), spec), out_specs=(spec, spec), check_vma=False
    )
```

```python
import math
import random

import jax
import jax.numpy as jnp
from jax import lax
from jax.experimental import pallas as pl
from jax.experimental.pallas import tpu as pltpu
from jax.sharding import PartitionSpec as P

MESH = pl.DeviceIdType.MESH
F32, BF16 = jnp.float32, jnp.bfloat16
NN = (((1,), (0,)), ((), ()))
NT = (((1,), (1,)), ((), ()))
N = 512
DEVICES = 128


def relative_groups():
    every = [(x, y, z) for x in range(4) for y in range(4) for z in range(2)]
    random.Random(0).shuffle(every)
    return [every[i : i + 4] for i in range(0, 32, 4)]


def halves(x):
    high = x.astype(BF16)
    return high, (x - high.astype(F32)).astype(BF16)


def dot3(left, right, dims=NN):
    def one(a, b):
        return lax.dot_general(a, b, dims, preferred_element_type=F32)

    return one(left[0], right[0]) + (one(left[0], right[1]) + one(left[1], right[0]))


def cos_sin(steps):
    quarter = (steps + 128) >> 8
    angle = (steps - quarter * 256).astype(F32) * (2.0 * math.pi / 1024)
    square = angle * angle
    cos = 1.0 / 40320 - square * (1.0 / 3628800)
    for term in (-1.0 / 720, 1.0 / 24, -0.5, 1.0):
        cos = term + square * cos
    sin = -1.0 / 5040 + square * (1.0 / 362880)
    for term in (1.0 / 120, -1.0 / 6, 1.0):
        sin = term + square * sin
    sin = angle * sin
    quarter = quarter & 3
    odd = (quarter & 1) == 1
    cos, sin = jnp.where(odd, sin, cos), jnp.where(odd, cos, sin)
    cos = jnp.where((quarter == 1) | (quarter == 2), -cos, cos)
    sin = jnp.where(quarter >= 2, -sin, sin)
    return cos, sin


def kernel(
    freq_ref, traces_ref, prim_ref,
    resid_out, pred_out, step_out,
    raw, xh, xl, th, tl, sbuf, rbuf, whole, ah, al, resid, pred, freqs, stat, slots,
    raw_sem, prim_sem, send_sem, recv_sem, own_sem, out_sem, stat_send, stat_recv,
):
    src, rcv = lax.axis_index("src"), lax.axis_index("rcv")
    me = src * 16 + rcv
    xs = [(rcv // 4 + d) % 4 for d in range(4)]
    ys = [(src // 2 + d) % 4 for d in range(4)]
    z_low = [(src + d) % 2 for d in range(2)]
    z_high = [(rcv // 2 + d) % 2 for d in range(2)]
    cores = [(rcv + d) % 2 for d in range(2)]
    groups = relative_groups()

    def targets(group):
        x, y, z = group
        return [
            (ys[y] * 2 + z_low[z], xs[x] * 4 + z_high[h] * 2 + cores[c])
            for h in range(2)
            for c in range(2)
            if (x, y, z, h, c) != (0, 0, 0, 0, 0)
        ]

    everyone = [to for bunch in groups for group in bunch for to in targets(group)]
    home = [k for k, bunch in enumerate(groups) if (0, 0, 0) in bunch][0]

    def load(b, g):
        rows = pl.ds(b * 4, 4)
        return pltpu.make_async_copy(traces_ref.at[g, rows], raw.at[rows, g], raw_sem.at[b])

    for b in range(4):
        for g in range(4):
            load(b, g).start()

    barrier = pltpu.get_barrier_semaphore()
    for to in everyone:
        pl.semaphore_signal(barrier, inc=1, device_id=to, device_id_type=MESH)

    lane = lax.broadcasted_iota(jnp.int32, (128, 128), 1)

    def table(j):
        for d in range(128):
            freqs[d : d + 1, :] = jnp.full((1, 128), freq_ref[2 * d + j], jnp.int32)
        freq = freqs[...]
        cos, sin = cos_sin((freq * lane) & 1023)
        cos, sin = cos * 0.03125, sin * 0.03125
        turn_cos, turn_sin = cos_sin((freq * 128) & 1023)
        sign = 1.0 - 2.0 * (freq & 1).astype(F32)
        for a in range(4):
            if a:
                cos, sin = cos * turn_cos - sin * turn_sin, sin * turn_cos + cos * turn_sin
            for c, part in enumerate((cos, -sin)):
                for k, value in ((a, part), (a + 4, part * sign)):
                    high, low = halves(value)
                    th[j, c * 128 : c * 128 + 128, k * 128 : k * 128 + 128] = high
                    tl[j, c * 128 : c * 128 + 128, k * 128 : k * 128 + 128] = low

    def transform(j, h, b):
        rows = pl.ds(pl.multiple_of((h * 2 + b) * 512, 512), 512)
        out = dot3((th[j], tl[j]), (xh[rows, :], xl[rows, :]), NT)
        for c in range(2):
            for d in range(0, 128, 8):
                for i in range(4):
                    start = ((j * 2 + h) * DEVICES + d) * 16 + c * 8 + b * 4 + i
                    sbuf[pl.ds(start, 8, stride=16), :] = out[
                        c * 128 + d : c * 128 + d + 8, i * 128 : i * 128 + 128
                    ]

    def piece(j, h, index, count=1):
        return pl.ds(pl.multiple_of(((j * 2 + h) * DEVICES + index) * 16, 16), 16 * count)

    def own(j, h):
        return pltpu.make_async_copy(sbuf.at[piece(j, h, me)], rbuf.at[piece(j, h, me)], own_sem.at[j * 2 + h])

    def send(j, h):
        own(j, h).start()
        for k, bunch in enumerate(groups):
            for group in bunch:
                for to in targets(group):
                    pltpu.make_async_remote_copy(
                        src_ref=sbuf.at[piece(j, h, to[0] * 16 + to[1])],
                        dst_ref=rbuf.at[piece(j, h, me)],
                        send_sem=send_sem.at[j * 2 + h],
                        recv_sem=recv_sem.at[(j * 2 + h) * 8 + k],
                        device_id=to,
                        device_id_type=MESH,
                    ).start()

    def arrival(j, h, k, count):
        return pltpu.make_async_remote_copy(
            src_ref=sbuf.at[piece(j, h, 0, count)],
            dst_ref=rbuf.at[piece(j, h, 0, count)],
            send_sem=send_sem.at[j * 2 + h],
            recv_sem=recv_sem.at[(j * 2 + h) * 8 + k],
            device_id=everyone[0],
            device_id_type=MESH,
        )

    table(0)
    for h in range(2):
        for b in range(2):
            n = h * 2 + b
            for g in range(4):
                load(n, g).wait()
            high, low = halves(raw[n * 4 : n * 4 + 4].reshape(512, 1024))
            xh[n * 512 : n * 512 + 512, :] = high
            xl[n * 512 : n * 512 + 512, :] = low
            transform(0, h, b)
        if h == 0:
            pl.semaphore_wait(barrier, DEVICES - 1)
        send(0, h)

    def prim_copy(j, c):
        return pltpu.make_async_copy(
            prim_ref.at[j, c], raw.at[pl.ds(4 * c, 4), :, :, pl.ds(j * N, N)], prim_sem.at[j * 2 + c]
        )

    for j in range(2):
        for c in range(2):
            prim_copy(j, c).start()

    table(1)
    for h in range(2):
        for b in range(2):
            transform(1, h, b)
        send(1, h)

    wide = lax.broadcasted_iota(jnp.int32, (16, 128), 1)
    odd, upper = (wide // 32) % 2 == 1, wide >= 64
    lanes = lax.broadcasted_iota(jnp.int32, (1, 128), 1)
    total = jnp.zeros((1, 128), F32)

    def put(slot, value):
        high, low = halves(value)
        rows, columns = slice(slot % 4 * N, slot % 4 * N + N), slice(slot // 4 * N, slot // 4 * N + N)
        xh[rows, columns] = high
        xl[rows, columns] = low

    def get(slot):
        rows, columns = slice(slot % 4 * N, slot % 4 * N + N), slice(slot // 4 * N, slot // 4 * N + N)
        return xh[rows, columns], xl[rows, columns]

    for j in range(2):
        for c in range(2):
            prim_copy(j, c).wait()
        model = [raw[4 * c : 4 * c + 4, :, :, j * N : j * N + N].reshape(N, N) for c in range(2)]
        for index, value in enumerate((model[0] + model[1], model[0], model[1])):
            high, low = halves(value)
            ah[index] = high
            al[index] = low

        @pl.loop(0, 2)
        def _(h):
            for k, bunch in enumerate(groups):
                if k == home:
                    own(j, h).wait()
                arrival(j, h, k, 15 if k == home else 16).wait_recv()
                for x, y, z in bunch:
                    from_x, from_s = xs[-x % 4], ys[-y % 4] * 2 + z_low[z]
                    v = [rbuf[piece(j, h, from_s * 16 + from_x * 4 + q), :] for q in range(4)]
                    for m in (0, 2):
                        a, b = v[m], v[m + 1]
                        v[m] = jnp.where(odd, pltpu.roll(b, 32, 1), a)
                        v[m + 1] = jnp.where(odd, b, pltpu.roll(a, 96, 1))
                    for m in (0, 1):
                        a, b = v[m], v[m + 2]
                        v[m] = jnp.where(upper, pltpu.roll(b, 64, 1), a)
                        v[m + 2] = jnp.where(upper, b, pltpu.roll(a, 64, 1))
                    columns = pl.ds(pl.multiple_of(from_x * 128, 128), 128)
                    for g in range(4):
                        rows = pl.ds(pl.multiple_of(from_s * 64 + g * 16 + h * 8, 8), 8)
                        whole[0, rows, columns] = v[g][:8]
                        whole[1, rows, columns] = v[g][8:]

        for p in range(4):
            for q in range(p, 4):
                a, b = slice(p * 128, p * 128 + 128), slice(q * 128, q * 128 + 128)
                parts = []
                for c in range(2):
                    value = 0.5 * (whole[c, a, b] + whole[c, b, a].T)
                    whole[c, a, b] = value
                    parts.append((value, value.T if p != q else None))
                for (rows, columns), t in (((a, b), 0), ((b, a), 1))[: 1 + (p != q)]:
                    re, im = parts[0][t], parts[1][t]
                    if t:
                        whole[0, rows, columns] = re
                        whole[1, rows, columns] = im
                    for index, value in enumerate((re, im - re, re + im, im)):
                        high, low = halves(value)
                        at = slice(index * N + rows.start, index * N + rows.stop)
                        xh[at, columns] = high
                        xl[at, columns] = low

        first = dot3((ah[0], al[0]), get(0))
        second = dot3((ah[1], al[1]), get(1))
        third = dot3((ah[2], al[2]), get(2))
        if j:
            for copy in out_copies(resid_out, pred_out, resid, pred, out_sem, 0):
                copy.wait()
        re = whole[0] - (first - third)
        im = whole[1] - (first + second)
        resid[0] = re
        resid[1] = im
        put(4, re + im)
        put(5, re)
        put(6, im)
        cross = -dot3(get(2), get(1))
        square = dot3(get(3), get(3))
        flipped = cross.T
        h_re = 0.5 * (cross + flipped) + 2.0 * square
        h_im = 0.5 * (flipped - cross)
        put(7, h_re)
        put(0, h_im - h_re)
        put(1, h_im + h_re)
        first = dot3(get(4), get(7))
        second = dot3(get(5), get(0))
        third = dot3(get(6), get(1))
        re = first - third
        im = first + second
        pred[0] = re
        pred[1] = im
        numer = jnp.sum(resid[0] * re + resid[1] * im, axis=0, keepdims=True)
        denom = jnp.sum(re * re + im * im, axis=0, keepdims=True)
        fold = []
        for value in (numer, denom):
            value = value[:, :128] + value[:, 128:256] + value[:, 256:384] + value[:, 384:]
            fold.append(value + pltpu.roll(value, 64, 1))
        weight = freq_ref[me * 2 + j].astype(F32) * (1.0 / 512)
        total += weight * jnp.where(lanes < 64, fold[0], fold[1])
        for copy in out_copies(resid_out, pred_out, resid, pred, out_sem, j):
            copy.start()

    stat[0] = total
    slots[me] = total
    for to in everyone:
        pltpu.make_async_remote_copy(
            src_ref=stat.at[0],
            dst_ref=slots.at[me],
            send_sem=stat_send,
            recv_sem=stat_recv,
            device_id=to,
            device_id_type=MESH,
        ).start()
    done = pltpu.make_async_remote_copy(
        src_ref=slots.at[pl.ds(0, 127)],
        dst_ref=slots.at[pl.ds(0, 127)],
        send_sem=stat_send,
        recv_sem=stat_recv,
        device_id=everyone[0],
        device_id_type=MESH,
    )
    for j in range(2):
        for h in range(2):
            arrival(j, h, 0, 127).wait_send()
    done.wait_recv()
    every = jnp.sum(slots[...], axis=0)
    numer = jnp.sum(jnp.where(lanes < 64, every, 0.0), axis=1, keepdims=True)
    denom = jnp.sum(jnp.where(lanes < 64, 0.0, every), axis=1, keepdims=True)
    step_out[...] = jnp.broadcast_to(numer / denom, (8, N))
    done.wait_send()
    for copy in out_copies(resid_out, pred_out, resid, pred, out_sem, 1):
        copy.wait()


def out_copies(resid_out, pred_out, resid, pred, sem, j):
    return (
        pltpu.make_async_copy(resid, resid_out.at[j], sem.at[j, 0]),
        pltpu.make_async_copy(pred, pred_out.at[j], sem.at[j, 1]),
    )


def on_device(traces, freq_index, primaries):
    samples = traces.shape[2]
    anywhere, vmem = pl.BlockSpec(memory_space=pl.ANY), pl.BlockSpec(memory_space=pltpu.VMEM)
    big = jax.ShapeDtypeStruct((2, 2, N, N), F32)
    dma = pltpu.SemaphoreType.DMA
    resid, pred, step = pl.pallas_call(
        kernel,
        out_shape=(big, big, jax.ShapeDtypeStruct((8, N), F32)),
        in_specs=[pl.BlockSpec(memory_space=pltpu.SMEM), anywhere, anywhere],
        out_specs=(anywhere, anywhere, vmem),
        scratch_shapes=[
            pltpu.VMEM((16, 4, 32, 1024), F32),
            pltpu.VMEM((2048, 1024), BF16),
            pltpu.VMEM((2048, 1024), BF16),
            pltpu.VMEM((2, 256, 1024), BF16),
            pltpu.VMEM((2, 256, 1024), BF16),
            pltpu.VMEM((4 * DEVICES * 16, 128), F32),
            pltpu.VMEM((4 * DEVICES * 16, 128), F32),
            pltpu.VMEM((2, N, N), F32),
            pltpu.VMEM((3, N, N), BF16),
            pltpu.VMEM((3, N, N), BF16),
            pltpu.VMEM((2, N, N), F32),
            pltpu.VMEM((2, N, N), F32),
            pltpu.VMEM((128, 128), jnp.int32),
            pltpu.VMEM((1, 1, 128), F32),
            pltpu.VMEM((DEVICES, 1, 128), F32),
            dma((4,)), dma((4,)), dma((4,)), dma((32,)), dma((4,)), dma((2, 2)), dma, dma,
        ],
        compiler_params=pltpu.CompilerParams(
            collective_id=0, has_side_effects=True, vmem_limit_bytes=44 * 2**20
        ),
    )(freq_index, traces.reshape(4, 16, 32, samples), primaries.reshape(2, 2, 4, 4, 32, N))
    tiles = (2, 2, N // 8, 8, N)
    update = resid.reshape(tiles) - step * pred.reshape(tiles)
    return (resid, update.reshape(resid.shape))


def solution(mesh):
    spec = P(("src", "rcv"), None, None, None)
    return jax.shard_map(
        on_device, mesh=mesh, in_specs=(P("src", "rcv", None), P(), spec), out_specs=(spec, spec), check_vma=False
    )
```

```python
import math
import random

import jax
import jax.numpy as jnp
from jax import lax
from jax.experimental import pallas as pl
from jax.experimental.pallas import tpu as pltpu
from jax.sharding import PartitionSpec as P

MESH = pl.DeviceIdType.MESH
F32, BF16 = jnp.float32, jnp.bfloat16
NN = (((1,), (0,)), ((), ()))
NT = (((1,), (1,)), ((), ()))
N = 512
DEVICES = 128


def far(x, y, z=0, h=0, c=0):
    return min(x, 4 - x) + min(y, 4 - y) + (0, 2, 1, 1)[2 * z + h]


def relative_groups():
    every = [(x, y, z) for x in range(4) for y in range(4) for z in range(2)]
    random.Random(0).shuffle(every)
    return [every[i : i + 4] for i in range(0, 32, 4)]


def halves(x):
    high = x.astype(BF16)
    return high, (x - high.astype(F32)).astype(BF16)


def dot3(left, right, dims=NN):
    def one(a, b):
        return lax.dot_general(a, b, dims, preferred_element_type=F32)

    return one(left[0], right[0]) + (one(left[0], right[1]) + one(left[1], right[0]))


def cos_sin(steps):
    quarter = (steps + 128) >> 8
    angle = (steps - quarter * 256).astype(F32) * (2.0 * math.pi / 1024)
    square = angle * angle
    cos = 1.0 / 40320 - square * (1.0 / 3628800)
    for term in (-1.0 / 720, 1.0 / 24, -0.5, 1.0):
        cos = term + square * cos
    sin = -1.0 / 5040 + square * (1.0 / 362880)
    for term in (1.0 / 120, -1.0 / 6, 1.0):
        sin = term + square * sin
    sin = angle * sin
    quarter = quarter & 3
    odd = (quarter & 1) == 1
    cos, sin = jnp.where(odd, sin, cos), jnp.where(odd, cos, sin)
    cos = jnp.where((quarter == 1) | (quarter == 2), -cos, cos)
    sin = jnp.where(quarter >= 2, -sin, sin)
    return cos, sin


def kernel(
    freq_hbm, traces_ref, prim_ref,
    resid_out, pred_out, step_out,
    raw, xh, xl, th, tl, sbuf, rbuf, whole, ah, al, resid, pred, freq_ref, freqs, stat, slots,
    freq_sem, raw_sem, prim_sem, send_sem, recv_sem, own_sem, out_sem, stat_send, stat_recv,
):
    src, rcv = lax.axis_index("src"), lax.axis_index("rcv")
    me = src * 16 + rcv
    xs = [(rcv // 4 + d) % 4 for d in range(4)]
    ys = [(src // 2 + d) % 4 for d in range(4)]
    z_low = [(src + d) % 2 for d in range(2)]
    z_high = [(rcv // 2 + d) % 2 for d in range(2)]
    cores = [(rcv + d) % 2 for d in range(2)]
    groups = relative_groups()

    def targets(group):
        x, y, z = group
        return [
            (ys[y] * 2 + z_low[z], xs[x] * 4 + z_high[h] * 2 + cores[c])
            for h in range(2)
            for c in range(2)
            if (x, y, z, h, c) != (0, 0, 0, 0, 0)
        ]

    offsets = [(x, y, z, h, c) for x in range(4) for y in range(4) for z in range(2) for h in range(2) for c in range(2)]
    offsets = sorted(offsets[1:], key=lambda offset: -far(*offset))
    everyone = [(ys[y] * 2 + z_low[z], xs[x] * 4 + z_high[h] * 2 + cores[c]) for x, y, z, h, c in offsets]
    home = [k for k, bunch in enumerate(groups) if (0, 0, 0) in bunch][0]

    def load(b, g):
        rows = pl.ds(b * 4, 4)
        return pltpu.make_async_copy(traces_ref.at[g, rows], raw.at[rows, g], raw_sem.at[b])

    freq_copy = pltpu.make_async_copy(freq_hbm, freq_ref, freq_sem)
    freq_copy.start()
    for b in range(4):
        for g in range(4):
            load(b, g).start()

    barrier = pltpu.get_barrier_semaphore()
    for to in everyone:
        pl.semaphore_signal(barrier, inc=1, device_id=to, device_id_type=MESH)

    lane = lax.broadcasted_iota(jnp.int32, (128, 128), 1)

    def table(j):
        for d in range(128):
            freqs[d : d + 1, :] = jnp.full((1, 128), freq_ref[2 * d + j], jnp.int32)
        freq = freqs[...]
        cos, sin = cos_sin((freq * lane) & 1023)
        cos, sin = cos * 0.03125, sin * 0.03125
        turn_cos, turn_sin = cos_sin((freq * 128) & 1023)
        sign = 1.0 - 2.0 * (freq & 1).astype(F32)
        for a in range(4):
            if a:
                cos, sin = cos * turn_cos - sin * turn_sin, sin * turn_cos + cos * turn_sin
            for c, part in enumerate((cos, -sin)):
                for k, value in ((a, part), (a + 4, part * sign)):
                    high, low = halves(value)
                    th[j, c * 128 : c * 128 + 128, k * 128 : k * 128 + 128] = high
                    tl[j, c * 128 : c * 128 + 128, k * 128 : k * 128 + 128] = low

    def transform(h, b):
        rows = slice((h * 2 + b) * 512, (h * 2 + b) * 512 + 512)
        out = dot3((th[0], tl[0]), (xh[rows, :], xl[rows, :]), NT)
        for c in range(2):
            for d in range(0, 128, 8):
                for i in range(4):
                    start = (h * DEVICES + d) * 16 + c * 8 + b * 4 + i
                    sbuf[pl.ds(start, 8, stride=16), :] = out[
                        c * 128 + d : c * 128 + d + 8, i * 128 : i * 128 + 128
                    ]

    def transform_part(c):
        @pl.loop(0, 4)
        def _(b):
            rows = pl.ds(pl.multiple_of(b * 512, 512), 512)
            part = slice(c * 128, c * 128 + 128)
            out = dot3((th[1, part], tl[1, part]), (xh[rows, :], xl[rows, :]), NT)
            for d in range(0, 128, 8):
                for i in range(4):
                    start = ((2 + c) * DEVICES + d) * 16 + b * 4 + i
                    sbuf[pl.ds(start, 8, stride=16), :] = out[d : d + 8, i * 128 : i * 128 + 128]

    def piece(j, h, index, count=1):
        return pl.ds(pl.multiple_of(((j * 2 + h) * DEVICES + index) * 16, 16), 16 * count)

    def own(j, h):
        return pltpu.make_async_copy(sbuf.at[piece(j, h, me)], rbuf.at[piece(j, h, me)], own_sem.at[j * 2 + h])

    def send(j, h):
        own(j, h).start()
        for k, bunch in enumerate(groups):
            for group in bunch:
                for to in targets(group):
                    pltpu.make_async_remote_copy(
                        src_ref=sbuf.at[piece(j, h, to[0] * 16 + to[1])],
                        dst_ref=rbuf.at[piece(j, h, me)],
                        send_sem=send_sem.at[j * 2 + h],
                        recv_sem=recv_sem.at[(j * 2 + h) * 8 + k],
                        device_id=to,
                        device_id_type=MESH,
                    ).start()

    def arrival(j, h, k, count):
        return pltpu.make_async_remote_copy(
            src_ref=sbuf.at[piece(j, h, 0, count)],
            dst_ref=rbuf.at[piece(j, h, 0, count)],
            send_sem=send_sem.at[j * 2 + h],
            recv_sem=recv_sem.at[(j * 2 + h) * 8 + k],
            device_id=everyone[0],
            device_id_type=MESH,
        )

    freq_copy.wait()
    table(0)
    for h in range(2):
        for b in range(2):
            n = h * 2 + b
            for g in range(4):
                load(n, g).wait()
            high, low = halves(raw[n * 4 : n * 4 + 4].reshape(512, 1024))
            xh[n * 512 : n * 512 + 512, :] = high
            xl[n * 512 : n * 512 + 512, :] = low
            transform(h, b)
        if h == 0:
            pl.semaphore_wait(barrier, DEVICES - 1)
        send(0, h)

    def prim_copy(j, c):
        return pltpu.make_async_copy(
            prim_ref.at[j, c], raw.at[pl.ds(4 * c, 4), :, :, pl.ds(j * N, N)], prim_sem.at[j * 2 + c]
        )

    for j in range(2):
        for c in range(2):
            prim_copy(j, c).start()

    table(1)
    for c in range(2):
        transform_part(c)
        send(1, c)

    wide = lax.broadcasted_iota(jnp.int32, (16, 128), 1)
    odd, upper = (wide // 32) % 2 == 1, wide >= 64
    lanes = lax.broadcasted_iota(jnp.int32, (1, 128), 1)
    total = jnp.zeros((1, 128), F32)

    def put(slot, value):
        high, low = halves(value)
        rows, columns = slice(slot % 4 * N, slot % 4 * N + N), slice(slot // 4 * N, slot // 4 * N + N)
        xh[rows, columns] = high
        xl[rows, columns] = low

    def get(slot):
        rows, columns = slice(slot % 4 * N, slot % 4 * N + N), slice(slot // 4 * N, slot // 4 * N + N)
        return xh[rows, columns], xl[rows, columns]

    def model_operands(j):
        for c in range(2):
            prim_copy(j, c).wait()
        model = [raw[4 * c : 4 * c + 4, :, :, j * N : j * N + N].reshape(N, N) for c in range(2)]
        for index, value in enumerate((model[0] + model[1], model[0], model[1])):
            high, low = halves(value)
            ah[index] = high
            al[index] = low

    def assemble(j, h, store):
        for k, bunch in enumerate(groups):
            if k == home:
                own(j, h).wait()
            arrival(j, h, k, 15 if k == home else 16).wait_recv()
            for x, y, z in bunch:
                from_x, from_s = xs[-x % 4], ys[-y % 4] * 2 + z_low[z]
                v = [rbuf[piece(j, h, from_s * 16 + from_x * 4 + q), :] for q in range(4)]
                for m in (0, 2):
                    a, b = v[m], v[m + 1]
                    v[m] = jnp.where(odd, pltpu.roll(b, 32, 1), a)
                    v[m + 1] = jnp.where(odd, b, pltpu.roll(a, 96, 1))
                for m in (0, 1):
                    a, b = v[m], v[m + 2]
                    v[m] = jnp.where(upper, pltpu.roll(b, 64, 1), a)
                    v[m + 2] = jnp.where(upper, b, pltpu.roll(a, 64, 1))
                columns = pl.ds(pl.multiple_of(from_x * 128, 128), 128)
                for g in range(4):
                    store(h, from_s * 64 + g * 16, columns, v[g])

    def store_both(h, row, columns, value):
        rows = pl.ds(pl.multiple_of(row + h * 8, 8), 8)
        whole[0, rows, columns] = value[:8]
        whole[1, rows, columns] = value[8:]

    def store_part(c, row, columns, value):
        whole[c, pl.ds(pl.multiple_of(row, 16), 16), columns] = value

    def symmetric(c, then):
        for p in range(4):
            for q in range(p, 4):
                a, b = slice(p * 128, p * 128 + 128), slice(q * 128, q * 128 + 128)
                value = 0.5 * (whole[c, a, b] + whole[c, b, a].T)
                whole[c, a, b] = value
                then(a, b, value)
                if p != q:
                    value = value.T
                    whole[c, b, a] = value
                    then(b, a, value)

    def put_block(slot, rows, columns, value):
        high, low = halves(value)
        at = slice(slot * N + rows.start, slot * N + rows.stop)
        xh[at, columns] = high
        xl[at, columns] = low

    def real_operands(rows, columns, value):
        put_block(0, rows, columns, value)

    def imag_operands(rows, columns, value):
        real = whole[0, rows, columns]
        put_block(1, rows, columns, value - real)
        put_block(2, rows, columns, real + value)
        put_block(3, rows, columns, value)

    for j in range(2):
        model_operands(j)
        if j == 0:

            @pl.loop(0, 2)
            def _(h):
                assemble(0, h, store_both)

            symmetric(0, real_operands)
            pred[0] = dot3((ah[0], al[0]), get(0))
        else:
            assemble(1, 0, store_part)
            symmetric(0, real_operands)
            for copy in out_copies(resid_out, pred_out, resid, pred, out_sem, 0):
                copy.wait()
            pred[0] = dot3((ah[0], al[0]), get(0))
            assemble(1, 1, store_part)
        symmetric(1, imag_operands)

        cross = -dot3(get(2), get(1))
        square = dot3(get(3), get(3))
        second = dot3((ah[1], al[1]), get(1))
        flipped = cross.T
        h_re = 0.5 * (cross + flipped) + 2.0 * square
        h_im = 0.5 * (flipped - cross)
        ah[0], al[0] = halves(h_re)
        put(7, h_im - h_re)
        put(0, h_im + h_re)
        im = whole[1] - (pred[0] + second)
        resid[1] = im
        put(6, im)
        third = dot3((ah[2], al[2]), get(2))
        re = whole[0] - (pred[0] - third)
        resid[0] = re
        put(5, re)
        put(4, re + im)
        third = dot3(get(6), get(0))
        second = dot3(get(5), get(7))
        first = dot3(get(4), (ah[0], al[0]))
        re = first - third
        im = first + second
        pred[0] = re
        pred[1] = im
        numer = jnp.sum(resid[0] * re + resid[1] * im, axis=0, keepdims=True)
        denom = jnp.sum(re * re + im * im, axis=0, keepdims=True)
        fold = []
        for value in (numer, denom):
            value = value[:, :128] + value[:, 128:256] + value[:, 256:384] + value[:, 384:]
            fold.append(value + pltpu.roll(value, 64, 1))
        weight = freq_ref[me * 2 + j].astype(F32) * (1.0 / 512)
        total += weight * jnp.where(lanes < 64, fold[0], fold[1])
        if j == 0:
            for copy in out_copies(resid_out, pred_out, resid, pred, out_sem, 0):
                copy.start()

    stat[0] = total
    slots[me] = total
    for to in everyone:
        pltpu.make_async_remote_copy(
            src_ref=stat.at[0],
            dst_ref=slots.at[me],
            send_sem=stat_send,
            recv_sem=stat_recv,
            device_id=to,
            device_id_type=MESH,
        ).start()
    for copy in out_copies(resid_out, pred_out, resid, pred, out_sem, 1):
        copy.start()
    done = pltpu.make_async_remote_copy(
        src_ref=slots.at[pl.ds(0, 127)],
        dst_ref=slots.at[pl.ds(0, 127)],
        send_sem=stat_send,
        recv_sem=stat_recv,
        device_id=everyone[0],
        device_id_type=MESH,
    )
    for j in range(2):
        for h in range(2):
            arrival(j, h, 0, 127).wait_send()
    done.wait_recv()
    every = jnp.sum(slots[...], axis=0)
    numer = jnp.sum(jnp.where(lanes < 64, every, 0.0), axis=1, keepdims=True)
    denom = jnp.sum(jnp.where(lanes < 64, 0.0, every), axis=1, keepdims=True)
    step_out[...] = jnp.broadcast_to(numer / denom, (8, N))
    done.wait_send()
    for copy in out_copies(resid_out, pred_out, resid, pred, out_sem, 1):
        copy.wait()


def out_copies(resid_out, pred_out, resid, pred, sem, j):
    return (
        pltpu.make_async_copy(resid, resid_out.at[j], sem.at[j, 0]),
        pltpu.make_async_copy(pred, pred_out.at[j], sem.at[j, 1]),
    )


def final_kernel(resid, pred, step, resid_out, next_out, new, resid_sem, next_sem):
    copies = []
    for j in range(2):
        for c in range(2):
            copies.append(pltpu.make_async_copy(resid.at[j, c], resid_out.at[j, c], resid_sem.at[j * 2 + c]))
            copies[-1].start()
            for half in range(2):
                rows = slice(half * 256, half * 256 + 256)
                value = resid[j, c, rows, :] - jnp.tile(step[...], (32, 1)) * pred[j, c, rows, :]
                new[j, c, rows, :] = value
                at = (j, c, pl.ds(half * 256, 256))
                copies.append(pltpu.make_async_copy(new.at[at], next_out.at[at], next_sem.at[j * 4 + c * 2 + half]))
                copies[-1].start()
    for copy in copies:
        copy.wait()


def on_device(traces, freq_index, primaries):
    samples = traces.shape[2]
    anywhere, vmem = pl.BlockSpec(memory_space=pl.ANY), pl.BlockSpec(memory_space=pltpu.VMEM)
    big = jax.ShapeDtypeStruct((2, 2, N, N), F32)
    dma = pltpu.SemaphoreType.DMA
    resid, pred, step = pl.pallas_call(
        kernel,
        out_shape=(big, big, jax.ShapeDtypeStruct((8, N), F32)),
        in_specs=[pl.BlockSpec(memory_space=pltpu.HBM), anywhere, anywhere],
        out_specs=(anywhere, anywhere, vmem),
        scratch_shapes=[
            pltpu.VMEM((16, 4, 32, 1024), F32),
            pltpu.VMEM((2048, 1024), BF16),
            pltpu.VMEM((2048, 1024), BF16),
            pltpu.VMEM((2, 256, 1024), BF16),
            pltpu.VMEM((2, 256, 1024), BF16),
            pltpu.VMEM((4 * DEVICES * 16, 128), F32),
            pltpu.VMEM((4 * DEVICES * 16, 128), F32),
            pltpu.VMEM((2, N, N), F32),
            pltpu.VMEM((3, N, N), BF16),
            pltpu.VMEM((3, N, N), BF16),
            pltpu.VMEM((2, N, N), F32),
            pltpu.VMEM((2, N, N), F32),
            pltpu.SMEM((256,), jnp.int32),
            pltpu.VMEM((128, 128), jnp.int32),
            pltpu.VMEM((1, 1, 128), F32),
            pltpu.VMEM((DEVICES, 1, 128), F32),
            dma, dma((4,)), dma((4,)), dma((4,)), dma((32,)), dma((4,)), dma((2, 2)), dma, dma,
        ],
        compiler_params=pltpu.CompilerParams(
            collective_id=0, has_side_effects=True, vmem_limit_bytes=44 * 2**20
        ),
    )(freq_index, traces.reshape(4, 16, 32, samples), primaries.reshape(2, 2, 4, 4, 32, N))
    return pl.pallas_call(
        final_kernel,
        out_shape=(big, big),
        in_specs=[vmem, vmem, vmem],
        out_specs=(anywhere, anywhere),
        scratch_shapes=[pltpu.VMEM((2, 2, N, N), F32), dma((4,)), dma((8,))],
        compiler_params=pltpu.CompilerParams(vmem_limit_bytes=16 * 2**20),
    )(resid, pred, step)


def solution(mesh):
    spec = P(("src", "rcv"), None, None, None)
    return jax.shard_map(
        on_device, mesh=mesh, in_specs=(P("src", "rcv", None), P(), spec), out_specs=(spec, spec), check_vma=False
    )
```

```python
import math
import random

import jax
import jax.numpy as jnp
from jax import lax
from jax.experimental import pallas as pl
from jax.experimental.pallas import tpu as pltpu
from jax.sharding import PartitionSpec as P

MESH = pl.DeviceIdType.MESH
F32, BF16 = jnp.float32, jnp.bfloat16
NN = (((1,), (0,)), ((), ()))
NT = (((1,), (1,)), ((), ()))
N = 512
DEVICES = 128


def far(x, y, z=0, h=0, c=0):
    return min(x, 4 - x) + min(y, 4 - y) + (0, 2, 1, 1)[2 * z + h]


def far_first():
    every = [(x, y, z, h, c) for x in range(4) for y in range(4) for z in range(2) for h in range(2) for c in range(2)]
    every = every[1:]
    random.Random(1).shuffle(every)
    return sorted(every, key=lambda offset: -far(*offset))


def relative_groups():
    every = [(x, y, z) for x in range(4) for y in range(4) for z in range(2)]
    random.Random(0).shuffle(every)
    return [every[i : i + 4] for i in range(0, 32, 4)]


def bunch_of(bunches, group):
    return [group in bunch for bunch in bunches].index(True)


def halves(x):
    high = x.astype(BF16)
    return high, (x - high.astype(F32)).astype(BF16)


def dot3(left, right, dims=NN):
    def one(a, b):
        return lax.dot_general(a, b, dims, preferred_element_type=F32)

    return one(left[0], right[0]) + (one(left[0], right[1]) + one(left[1], right[0]))


def cos_sin(steps):
    quarter = (steps + 128) >> 8
    angle = (steps - quarter * 256).astype(F32) * (2.0 * math.pi / 1024)
    square = angle * angle
    cos = 1.0 / 40320 - square * (1.0 / 3628800)
    for term in (-1.0 / 720, 1.0 / 24, -0.5, 1.0):
        cos = term + square * cos
    sin = -1.0 / 5040 + square * (1.0 / 362880)
    for term in (1.0 / 120, -1.0 / 6, 1.0):
        sin = term + square * sin
    sin = angle * sin
    quarter = quarter & 3
    odd = (quarter & 1) == 1
    cos, sin = jnp.where(odd, sin, cos), jnp.where(odd, cos, sin)
    cos = jnp.where((quarter == 1) | (quarter == 2), -cos, cos)
    sin = jnp.where(quarter >= 2, -sin, sin)
    return cos, sin


def kernel(
    freq_hbm, traces_ref, prim_ref,
    resid_out, pred_out, step_out,
    raw, xh, xl, th, tl, sbuf, rbuf, whole, ah, al, resid, pred, freq_ref, freqs, stat, slots,
    freq_sem, raw_sem, prim_sem, send_sem, recv_sem, own_sem, out_sem, stat_send, stat_recv,
):
    src, rcv = lax.axis_index("src"), lax.axis_index("rcv")
    me = src * 16 + rcv
    xs = [(rcv // 4 + d) % 4 for d in range(4)]
    ys = [(src // 2 + d) % 4 for d in range(4)]
    z_low = [(src + d) % 2 for d in range(2)]
    z_high = [(rcv // 2 + d) % 2 for d in range(2)]
    cores = [(rcv + d) % 2 for d in range(2)]
    groups = relative_groups()

    offsets = far_first()
    order = [offset for bunch in groups for group in bunch for offset in sorted(offsets) if offset[:3] == group]

    def target(offset):
        x, y, z, h, c = offset
        return ys[y] * 2 + z_low[z], xs[x] * 4 + z_high[h] * 2 + cores[c]

    everyone = [target(offset) for offset in offsets]
    home = bunch_of(groups, (0, 0, 0))

    def load(b, g):
        rows = pl.ds(b * 4, 4)
        return pltpu.make_async_copy(traces_ref.at[g, rows], raw.at[rows, g], raw_sem.at[b])

    freq_copy = pltpu.make_async_copy(freq_hbm, freq_ref, freq_sem)
    freq_copy.start()
    for b in range(4):
        for g in range(4):
            load(b, g).start()

    barrier = pltpu.get_barrier_semaphore()
    for to in everyone:
        pl.semaphore_signal(barrier, inc=1, device_id=to, device_id_type=MESH)

    lane = lax.broadcasted_iota(jnp.int32, (128, 128), 1)

    def table(j):
        for d in range(128):
            freqs[d : d + 1, :] = jnp.full((1, 128), freq_ref[2 * d + j], jnp.int32)
        freq = freqs[...]
        cos, sin = cos_sin((freq * lane) & 1023)
        cos, sin = cos * 0.03125, sin * 0.03125
        turn_cos, turn_sin = cos_sin((freq * 128) & 1023)
        sign = 1.0 - 2.0 * (freq & 1).astype(F32)
        for a in range(4):
            if a:
                cos, sin = cos * turn_cos - sin * turn_sin, sin * turn_cos + cos * turn_sin
            for c, part in enumerate((cos, -sin)):
                for k, value in ((a, part), (a + 4, part * sign)):
                    high, low = halves(value)
                    th[j, c * 128 : c * 128 + 128, k * 128 : k * 128 + 128] = high
                    tl[j, c * 128 : c * 128 + 128, k * 128 : k * 128 + 128] = low

    def transform(h, b):
        rows = slice((h * 2 + b) * 512, (h * 2 + b) * 512 + 512)
        out = dot3((th[0], tl[0]), (xh[rows, :], xl[rows, :]), NT)
        for c in range(2):
            for d in range(0, 128, 8):
                for i in range(4):
                    start = (h * DEVICES + d) * 16 + c * 8 + b * 4 + i
                    sbuf[pl.ds(start, 8, stride=16), :] = out[
                        c * 128 + d : c * 128 + d + 8, i * 128 : i * 128 + 128
                    ]

    def transform_part(c):
        @pl.loop(0, 4)
        def _(b):
            rows = pl.ds(pl.multiple_of(b * 512, 512), 512)
            part = slice(c * 128, c * 128 + 128)
            out = dot3((th[1, part], tl[1, part]), (xh[rows, :], xl[rows, :]), NT)
            for d in range(0, 128, 8):
                for i in range(4):
                    start = ((2 + c) * DEVICES + d) * 16 + b * 4 + i
                    sbuf[pl.ds(start, 8, stride=16), :] = out[d : d + 8, i * 128 : i * 128 + 128]

    def piece(j, h, index, count=1):
        return pl.ds(pl.multiple_of(((j * 2 + h) * DEVICES + index) * 16, 16), 16 * count)

    def own(j, h):
        return pltpu.make_async_copy(sbuf.at[piece(j, h, me)], rbuf.at[piece(j, h, me)], own_sem.at[j * 2 + h])

    def send(j, h):
        own(j, h).start()
        for offset in order:
            to, k = target(offset), bunch_of(groups, offset[:3])
            pltpu.make_async_remote_copy(
                src_ref=sbuf.at[piece(j, h, to[0] * 16 + to[1])],
                dst_ref=rbuf.at[piece(j, h, me)],
                send_sem=send_sem.at[j * 2 + h],
                recv_sem=recv_sem.at[(j * 2 + h) * 8 + k],
                device_id=to,
                device_id_type=MESH,
            ).start()

    def arrival(j, h, k, count):
        return pltpu.make_async_remote_copy(
            src_ref=sbuf.at[piece(j, h, 0, count)],
            dst_ref=rbuf.at[piece(j, h, 0, count)],
            send_sem=send_sem.at[j * 2 + h],
            recv_sem=recv_sem.at[(j * 2 + h) * 8 + k],
            device_id=everyone[0],
            device_id_type=MESH,
        )

    freq_copy.wait()
    table(0)
    for h in range(2):
        for b in range(2):
            n = h * 2 + b
            for g in range(4):
                load(n, g).wait()
            high, low = halves(raw[n * 4 : n * 4 + 4].reshape(512, 1024))
            xh[n * 512 : n * 512 + 512, :] = high
            xl[n * 512 : n * 512 + 512, :] = low
            transform(h, b)
        if h == 0:
            pl.semaphore_wait(barrier, DEVICES - 1)
        send(0, h)

    def prim_copy(j, c):
        return pltpu.make_async_copy(
            prim_ref.at[j, c], raw.at[pl.ds(4 * c, 4), :, :, pl.ds(j * N, N)], prim_sem.at[j * 2 + c]
        )

    for j in range(2):
        for c in range(2):
            prim_copy(j, c).start()

    table(1)
    for c in range(2):
        transform_part(c)
        send(1, c)

    wide = lax.broadcasted_iota(jnp.int32, (16, 128), 1)
    odd, upper = (wide // 32) % 2 == 1, wide >= 64
    lanes = lax.broadcasted_iota(jnp.int32, (1, 128), 1)
    total = jnp.zeros((1, 128), F32)

    def place(slot, rows=slice(0, N)):
        base = slot % 4 * N
        return slice(base + rows.start, base + rows.stop), slice(slot // 4 * N, slot // 4 * N + N)

    def put_rows(slot, rows, value):
        at = place(slot, rows)
        xh[at], xl[at] = halves(value)

    def get(slot, rows=slice(0, N)):
        at = place(slot, rows)
        return xh[at], xl[at]

    def model_operands(j):
        for c in range(2):
            prim_copy(j, c).wait()
        model = [raw[4 * c : 4 * c + 4, :, :, j * N : j * N + N].reshape(N, N) for c in range(2)]
        for index, value in enumerate((model[0] + model[1], model[0], model[1])):
            high, low = halves(value)
            ah[index] = high
            al[index] = low

    def assemble(j, h, store):
        for k, bunch in enumerate(groups):
            if k == home:
                own(j, h).wait()
            arrival(j, h, k, 15 if k == home else 16).wait_recv()
            for x, y, z in bunch:
                from_x, from_s = xs[-x % 4], ys[-y % 4] * 2 + z_low[z]
                v = [rbuf[piece(j, h, from_s * 16 + from_x * 4 + q), :] for q in range(4)]
                for m in (0, 2):
                    a, b = v[m], v[m + 1]
                    v[m] = jnp.where(odd, pltpu.roll(b, 32, 1), a)
                    v[m + 1] = jnp.where(odd, b, pltpu.roll(a, 96, 1))
                for m in (0, 1):
                    a, b = v[m], v[m + 2]
                    v[m] = jnp.where(upper, pltpu.roll(b, 64, 1), a)
                    v[m + 2] = jnp.where(upper, b, pltpu.roll(a, 64, 1))
                columns = pl.ds(pl.multiple_of(from_x * 128, 128), 128)
                for g in range(4):
                    store(h, from_s * 64 + g * 16, columns, v[g])

    def store_both(h, row, columns, value):
        rows = pl.ds(pl.multiple_of(row + h * 8, 8), 8)
        whole[0, rows, columns] = value[:8]
        whole[1, rows, columns] = value[8:]

    def store_part(c, row, columns, value):
        whole[c, pl.ds(pl.multiple_of(row, 16), 16), columns] = value

    def symmetric(c, then):
        for p in range(4):
            for q in range(p, 4):
                a, b = slice(p * 128, p * 128 + 128), slice(q * 128, q * 128 + 128)
                value = 0.5 * (whole[c, a, b] + whole[c, b, a].T)
                whole[c, a, b] = value
                then(a, b, value)
                if p != q:
                    value = value.T
                    whole[c, b, a] = value
                    then(b, a, value)

    def put_block(slot, rows, columns, value):
        high, low = halves(value)
        at = slice(slot * N + rows.start, slot * N + rows.stop)
        xh[at, columns] = high
        xl[at, columns] = low

    def real_operands(rows, columns, value):
        put_block(0, rows, columns, value)

    def imag_operands(rows, columns, value):
        real = whole[0, rows, columns]
        put_block(1, rows, columns, value - real)
        put_block(2, rows, columns, real + value)
        put_block(3, rows, columns, value)

    for j in range(2):
        model_operands(j)
        if j == 0:

            @pl.loop(0, 2)
            def _(h):
                assemble(0, h, store_both)

            symmetric(0, real_operands)
            pred[0] = dot3((ah[0], al[0]), get(0))
        else:
            assemble(1, 0, store_part)
            symmetric(0, real_operands)
            for copy in out_copies(resid_out, pred_out, resid, pred, out_sem, 0):
                copy.wait()
            pred[0] = dot3((ah[0], al[0]), get(0))
            assemble(1, 1, store_part)
        symmetric(1, imag_operands)

        cross = -dot3(get(2), get(1))
        high, low = get(3)
        square = lax.dot_general(high, high, NN, preferred_element_type=F32)
        mixed = lax.dot_general(high, low, NN, preferred_element_type=F32)
        second = dot3((ah[1], al[1]), get(1))
        flipped = cross.T
        h_re = 0.5 * (cross + flipped) + 2.0 * (square + (mixed + mixed.T))
        h_im = 0.5 * (flipped - cross)
        ah[0], al[0] = halves(h_re)
        put_rows(7, slice(0, N), h_im - h_re)
        put_rows(0, slice(0, N), h_im + h_re)
        resid[1] = whole[1] - (pred[0] + second)
        for half in range(2):
            rows = slice(half * 256, half * 256 + 256)
            third = dot3((ah[2, rows], al[2, rows]), get(2))
            re = whole[0, rows] - (pred[0, rows] - third)
            im = resid[1, rows]
            resid[0, rows] = re
            put_rows(4, rows, re + im)
            put_rows(5, rows, re)
            put_rows(6, rows, im)
        sums = []
        for half in range(2):
            rows = slice(half * 256, half * 256 + 256)
            third = dot3(get(6, rows), get(0))
            second = dot3(get(5, rows), get(7))
            first = dot3(get(4, rows), (ah[0], al[0]))
            re = first - third
            im = first + second
            pred[0, rows] = re
            pred[1, rows] = im
            numer = jnp.sum(resid[0, rows] * re + resid[1, rows] * im, axis=0, keepdims=True)
            denom = jnp.sum(re * re + im * im, axis=0, keepdims=True)
            sums.append((numer, denom))
        fold = []
        for value in (sums[0][0] + sums[1][0], sums[0][1] + sums[1][1]):
            value = value[:, :128] + value[:, 128:256] + value[:, 256:384] + value[:, 384:]
            fold.append(value + pltpu.roll(value, 64, 1))
        weight = freq_ref[me * 2 + j].astype(F32) * (1.0 / 512)
        total += weight * jnp.where(lanes < 64, fold[0], fold[1])
        if j == 0:
            for copy in out_copies(resid_out, pred_out, resid, pred, out_sem, 0):
                copy.start()

    stat[0] = total
    slots[me] = total
    for to in everyone:
        pltpu.make_async_remote_copy(
            src_ref=stat.at[0],
            dst_ref=slots.at[me],
            send_sem=stat_send,
            recv_sem=stat_recv,
            device_id=to,
            device_id_type=MESH,
        ).start()
    for copy in out_copies(resid_out, pred_out, resid, pred, out_sem, 1):
        copy.start()
    done = pltpu.make_async_remote_copy(
        src_ref=slots.at[pl.ds(0, 127)],
        dst_ref=slots.at[pl.ds(0, 127)],
        send_sem=stat_send,
        recv_sem=stat_recv,
        device_id=everyone[0],
        device_id_type=MESH,
    )
    for j in range(2):
        for h in range(2):
            arrival(j, h, 0, 127).wait_send()
    done.wait_recv()
    every = jnp.sum(slots[...], axis=0)
    numer = jnp.sum(jnp.where(lanes < 64, every, 0.0), axis=1, keepdims=True)
    denom = jnp.sum(jnp.where(lanes < 64, 0.0, every), axis=1, keepdims=True)
    step_out[...] = jnp.broadcast_to(numer / denom, (8, N))
    done.wait_send()
    for copy in out_copies(resid_out, pred_out, resid, pred, out_sem, 1):
        copy.wait()


def out_copies(resid_out, pred_out, resid, pred, sem, j):
    return (
        pltpu.make_async_copy(resid, resid_out.at[j], sem.at[j, 0]),
        pltpu.make_async_copy(pred, pred_out.at[j], sem.at[j, 1]),
    )


def final_kernel(resid, pred, step, resid_out, next_out, new, resid_sem, next_sem):
    copies = []
    for j in range(2):
        for c in range(2):
            copies.append(pltpu.make_async_copy(resid.at[j, c], resid_out.at[j, c], resid_sem.at[j * 2 + c]))
            copies[-1].start()
            for half in range(2):
                rows = slice(half * 256, half * 256 + 256)
                value = resid[j, c, rows, :] - jnp.tile(step[...], (32, 1)) * pred[j, c, rows, :]
                new[j, c, rows, :] = value
                at = (j, c, pl.ds(half * 256, 256))
                copies.append(pltpu.make_async_copy(new.at[at], next_out.at[at], next_sem.at[j * 4 + c * 2 + half]))
                copies[-1].start()
    for copy in copies:
        copy.wait()


def on_device(traces, freq_index, primaries):
    samples = traces.shape[2]
    anywhere, vmem = pl.BlockSpec(memory_space=pl.ANY), pl.BlockSpec(memory_space=pltpu.VMEM)
    big = jax.ShapeDtypeStruct((2, 2, N, N), F32)
    dma = pltpu.SemaphoreType.DMA
    resid, pred, step = pl.pallas_call(
        kernel,
        out_shape=(big, big, jax.ShapeDtypeStruct((8, N), F32)),
        in_specs=[pl.BlockSpec(memory_space=pltpu.HBM), anywhere, anywhere],
        out_specs=(anywhere, anywhere, vmem),
        scratch_shapes=[
            pltpu.VMEM((16, 4, 32, 1024), F32),
            pltpu.VMEM((2048, 1024), BF16),
            pltpu.VMEM((2048, 1024), BF16),
            pltpu.VMEM((2, 256, 1024), BF16),
            pltpu.VMEM((2, 256, 1024), BF16),
            pltpu.VMEM((4 * DEVICES * 16, 128), F32),
            pltpu.VMEM((4 * DEVICES * 16, 128), F32),
            pltpu.VMEM((2, N, N), F32),
            pltpu.VMEM((3, N, N), BF16),
            pltpu.VMEM((3, N, N), BF16),
            pltpu.VMEM((2, N, N), F32),
            pltpu.VMEM((2, N, N), F32),
            pltpu.SMEM((256,), jnp.int32),
            pltpu.VMEM((128, 128), jnp.int32),
            pltpu.VMEM((1, 1, 128), F32),
            pltpu.VMEM((DEVICES, 1, 128), F32),
            dma, dma((4,)), dma((4,)), dma((4,)), dma((32,)), dma((4,)), dma((2, 2)), dma, dma,
        ],
        compiler_params=pltpu.CompilerParams(
            collective_id=0, has_side_effects=True, vmem_limit_bytes=44 * 2**20
        ),
    )(pltpu.with_memory_space_constraint(freq_index, pltpu.HBM), traces.reshape(4, 16, 32, samples), primaries.reshape(2, 2, 4, 4, 32, N))
    return pl.pallas_call(
        final_kernel,
        out_shape=(big, big),
        in_specs=[vmem, vmem, vmem],
        out_specs=(anywhere, anywhere),
        scratch_shapes=[pltpu.VMEM((2, 2, N, N), F32), dma((4,)), dma((8,))],
        compiler_params=pltpu.CompilerParams(vmem_limit_bytes=16 * 2**20),
    )(resid, pred, step)


def solution(mesh):
    spec = P(("src", "rcv"), None, None, None)
    return jax.shard_map(
        on_device, mesh=mesh, in_specs=(P("src", "rcv", None), P(), spec), out_specs=(spec, spec), check_vma=False
    )
```

```python
import math
import random

import jax
import jax.numpy as jnp
from jax import lax
from jax.experimental import pallas as pl
from jax.experimental.pallas import tpu as pltpu
from jax.sharding import PartitionSpec as P

MESH = pl.DeviceIdType.MESH
F32, BF16 = jnp.float32, jnp.bfloat16
NN = (((1,), (0,)), ((), ()))
NT = (((1,), (1,)), ((), ()))
N = 512
DEVICES = 128


def far(x, y, z=0, h=0, c=0):
    return min(x, 4 - x) + min(y, 4 - y) + (0, 2, 1, 1)[2 * z + h]


def far_first():
    every = [(x, y, z, h, c) for x in range(4) for y in range(4) for z in range(2) for h in range(2) for c in range(2)]
    every = every[1:]
    random.Random(1).shuffle(every)
    return sorted(every, key=lambda offset: -far(*offset))


def relative_groups():
    every = [(x, y, z) for x in range(4) for y in range(4) for z in range(2)]
    random.Random(0).shuffle(every)
    return [every[i : i + 4] for i in range(0, 32, 4)]


def bunch_of(bunches, group):
    return [group in bunch for bunch in bunches].index(True)


def halves(x):
    high = x.astype(BF16)
    return high, (x - high.astype(F32)).astype(BF16)


def dot3(left, right, dims=NN):
    def one(a, b):
        return lax.dot_general(a, b, dims, preferred_element_type=F32)

    return one(left[0], right[0]) + (one(left[0], right[1]) + one(left[1], right[0]))


def cos_sin(steps):
    quarter = (steps + 128) >> 8
    angle = (steps - quarter * 256).astype(F32) * (2.0 * math.pi / 1024)
    square = angle * angle
    cos = 1.0 / 40320 - square * (1.0 / 3628800)
    for term in (-1.0 / 720, 1.0 / 24, -0.5, 1.0):
        cos = term + square * cos
    sin = -1.0 / 5040 + square * (1.0 / 362880)
    for term in (1.0 / 120, -1.0 / 6, 1.0):
        sin = term + square * sin
    sin = angle * sin
    quarter = quarter & 3
    odd = (quarter & 1) == 1
    cos, sin = jnp.where(odd, sin, cos), jnp.where(odd, cos, sin)
    cos = jnp.where((quarter == 1) | (quarter == 2), -cos, cos)
    sin = jnp.where(quarter >= 2, -sin, sin)
    return cos, sin


def kernel(
    freq_hbm, traces_ref, prim_ref,
    resid_out, pred_out, step_out,
    raw, xh, xl, th, tl, sbuf, rbuf, whole, ah, al, resid, pred, freq_ref, freqs, stat, slots,
    freq_sem, raw_sem, prim_sem, send_sem, recv_sem, own_sem, out_sem, stat_send, stat_recv,
):
    src, rcv = lax.axis_index("src"), lax.axis_index("rcv")
    me = src * 16 + rcv
    xs = [(rcv // 4 + d) % 4 for d in range(4)]
    ys = [(src // 2 + d) % 4 for d in range(4)]
    z_low = [(src + d) % 2 for d in range(2)]
    z_high = [(rcv // 2 + d) % 2 for d in range(2)]
    cores = [(rcv + d) % 2 for d in range(2)]
    groups = relative_groups()

    offsets = far_first()
    order = [offset for bunch in groups for group in bunch for offset in sorted(offsets) if offset[:3] == group]

    def target(offset):
        x, y, z, h, c = offset
        return ys[y] * 2 + z_low[z], xs[x] * 4 + z_high[h] * 2 + cores[c]

    everyone = [target(offset) for offset in offsets]
    home = bunch_of(groups, (0, 0, 0))

    def load(b, g):
        rows = pl.ds(b * 4, 4)
        return pltpu.make_async_copy(traces_ref.at[g, rows], raw.at[rows, g], raw_sem.at[b])

    freq_copy = pltpu.make_async_copy(freq_hbm, freq_ref, freq_sem)
    freq_copy.start()
    for b in range(4):
        for g in range(4):
            load(b, g).start()

    barrier = pltpu.get_barrier_semaphore()
    for to in everyone:
        pl.semaphore_signal(barrier, inc=1, device_id=to, device_id_type=MESH)

    lane = lax.broadcasted_iota(jnp.int32, (128, 128), 1)

    def table(j):
        for d in range(128):
            freqs[d : d + 1, :] = jnp.full((1, 128), freq_ref[2 * d + j], jnp.int32)
        freq = freqs[...]
        cos, sin = cos_sin((freq * lane) & 1023)
        cos, sin = cos * 0.03125, sin * 0.03125
        turn_cos, turn_sin = cos_sin((freq * 128) & 1023)
        sign = 1.0 - 2.0 * (freq & 1).astype(F32)
        for a in range(4):
            if a:
                cos, sin = cos * turn_cos - sin * turn_sin, sin * turn_cos + cos * turn_sin
            for c, part in enumerate((cos, -sin)):
                for k, value in ((a, part), (a + 4, part * sign)):
                    high, low = halves(value)
                    th[j, c * 128 : c * 128 + 128, k * 128 : k * 128 + 128] = high
                    tl[j, c * 128 : c * 128 + 128, k * 128 : k * 128 + 128] = low

    def transform(h, b):
        rows = slice((h * 2 + b) * 512, (h * 2 + b) * 512 + 512)
        out = dot3((th[0], tl[0]), (xh[rows, :], xl[rows, :]), NT)
        for c in range(2):
            for d in range(0, 128, 8):
                for i in range(4):
                    start = (h * DEVICES + d) * 16 + c * 8 + b * 4 + i
                    sbuf[pl.ds(start, 8, stride=16), :] = out[
                        c * 128 + d : c * 128 + d + 8, i * 128 : i * 128 + 128
                    ]

    def transform_part(c):
        @pl.loop(0, 4)
        def _(b):
            rows = pl.ds(pl.multiple_of(b * 512, 512), 512)
            part = slice(c * 128, c * 128 + 128)
            out = dot3((th[1, part], tl[1, part]), (xh[rows, :], xl[rows, :]), NT)
            for d in range(0, 128, 8):
                for i in range(4):
                    start = ((2 + c) * DEVICES + d) * 16 + b * 4 + i
                    sbuf[pl.ds(start, 8, stride=16), :] = out[d : d + 8, i * 128 : i * 128 + 128]

    def piece(j, h, index, count=1):
        return pl.ds(pl.multiple_of(((j * 2 + h) * DEVICES + index) * 16, 16), 16 * count)

    def own(j, h):
        return pltpu.make_async_copy(sbuf.at[piece(j, h, me)], rbuf.at[piece(j, h, me)], own_sem.at[j * 2 + h])

    def send(j, h):
        own(j, h).start()
        for offset in order:
            to, k = target(offset), bunch_of(groups, offset[:3])
            pltpu.make_async_remote_copy(
                src_ref=sbuf.at[piece(j, h, to[0] * 16 + to[1])],
                dst_ref=rbuf.at[piece(j, h, me)],
                send_sem=send_sem.at[j * 2 + h],
                recv_sem=recv_sem.at[(j * 2 + h) * 8 + k],
                device_id=to,
                device_id_type=MESH,
            ).start()

    def arrival(j, h, k, count):
        return pltpu.make_async_remote_copy(
            src_ref=sbuf.at[piece(j, h, 0, count)],
            dst_ref=rbuf.at[piece(j, h, 0, count)],
            send_sem=send_sem.at[j * 2 + h],
            recv_sem=recv_sem.at[(j * 2 + h) * 8 + k],
            device_id=everyone[0],
            device_id_type=MESH,
        )

    freq_copy.wait()
    table(0)
    for h in range(2):
        for b in range(2):
            n = h * 2 + b
            for g in range(4):
                load(n, g).wait()
            high, low = halves(raw[n * 4 : n * 4 + 4].reshape(512, 1024))
            xh[n * 512 : n * 512 + 512, :] = high
            xl[n * 512 : n * 512 + 512, :] = low
            transform(h, b)
        if h == 0:
            pl.semaphore_wait(barrier, DEVICES - 1)
        send(0, h)

    def prim_copy(j, c):
        return pltpu.make_async_copy(
            prim_ref.at[j, c], raw.at[pl.ds(4 * c, 4), :, :, pl.ds(j * N, N)], prim_sem.at[j * 2 + c]
        )

    for j in range(2):
        for c in range(2):
            prim_copy(j, c).start()

    table(1)
    for c in range(2):
        transform_part(c)
        send(1, c)

    wide = lax.broadcasted_iota(jnp.int32, (16, 128), 1)
    odd, upper = (wide // 32) % 2 == 1, wide >= 64
    lanes = lax.broadcasted_iota(jnp.int32, (1, 128), 1)
    total = jnp.zeros((1, 128), F32)

    def place(slot, rows=slice(0, N)):
        base = slot % 4 * N
        return slice(base + rows.start, base + rows.stop), slice(slot // 4 * N, slot // 4 * N + N)

    def put_rows(slot, rows, value):
        at = place(slot, rows)
        xh[at], xl[at] = halves(value)

    def get(slot, rows=slice(0, N)):
        at = place(slot, rows)
        return xh[at], xl[at]

    def model_operands(j):
        for c in range(2):
            prim_copy(j, c).wait()
        model = [raw[4 * c : 4 * c + 4, :, :, j * N : j * N + N].reshape(N, N) for c in range(2)]
        for index, value in enumerate(model):
            ah[index], al[index] = halves(value)

    def assemble(j, h, store):
        for k, bunch in enumerate(groups):
            if k == home:
                own(j, h).wait()
            arrival(j, h, k, 15 if k == home else 16).wait_recv()
            for x, y, z in bunch:
                from_x, from_s = xs[-x % 4], ys[-y % 4] * 2 + z_low[z]
                v = [rbuf[piece(j, h, from_s * 16 + from_x * 4 + q), :] for q in range(4)]
                for m in (0, 2):
                    a, b = v[m], v[m + 1]
                    v[m] = jnp.where(odd, pltpu.roll(b, 32, 1), a)
                    v[m + 1] = jnp.where(odd, b, pltpu.roll(a, 96, 1))
                for m in (0, 1):
                    a, b = v[m], v[m + 2]
                    v[m] = jnp.where(upper, pltpu.roll(b, 64, 1), a)
                    v[m + 2] = jnp.where(upper, b, pltpu.roll(a, 64, 1))
                columns = pl.ds(pl.multiple_of(from_x * 128, 128), 128)
                for g in range(4):
                    store(h, from_s * 64 + g * 16, columns, v[g])

    def store_both(h, row, columns, value):
        rows = pl.ds(pl.multiple_of(row + h * 8, 8), 8)
        whole[0, rows, columns] = value[:8]
        whole[1, rows, columns] = value[8:]

    def store_part(c, row, columns, value):
        whole[c, pl.ds(pl.multiple_of(row, 16), 16), columns] = value

    def symmetric(c, then):
        for p in range(4):
            for q in range(p, 4):
                a, b = slice(p * 128, p * 128 + 128), slice(q * 128, q * 128 + 128)
                value = 0.5 * (whole[c, a, b] + whole[c, b, a].T)
                whole[c, a, b] = value
                then(a, b, value)
                if p != q:
                    value = value.T
                    whole[c, b, a] = value
                    then(b, a, value)

    def put_block(slot, rows, columns, value):
        high, low = halves(value)
        at = slice(slot * N + rows.start, slot * N + rows.stop)
        xh[at, columns] = high
        xl[at, columns] = low

    def real_operands(rows, columns, value):
        put_block(0, rows, columns, value)

    def imag_operands(rows, columns, value):
        put_block(1, rows, columns, value)

    def gram(matrix):
        high, low = matrix
        square = lax.dot_general(high, high, NN, preferred_element_type=F32)
        mixed = lax.dot_general(high, low, NN, preferred_element_type=F32)
        return square + (mixed + mixed.T)

    def real_products():
        real = get(0)
        resid[0] = whole[0] - dot3((ah[0], al[0]), real)
        resid[1] = dot3((ah[1], al[1]), real)
        pred[0] = gram(real)

    for j in range(2):
        model_operands(j)
        if j == 0:

            @pl.loop(0, 2)
            def _(h):
                assemble(0, h, store_both)

            symmetric(0, real_operands)
            real_products()
        else:
            assemble(1, 0, store_part)
            symmetric(0, real_operands)
            for copy in out_copies(resid_out, pred_out, resid, pred, out_sem, 0):
                copy.wait()
            real_products()
            assemble(1, 1, store_part)
        symmetric(1, imag_operands)

        imag = get(1)
        cross = dot3(get(0), imag)
        h_re = pred[0] + gram(imag)
        h_im = cross - cross.T
        put_rows(2, slice(0, N), h_re)
        put_rows(3, slice(0, N), h_im - h_re)
        put_rows(7, slice(0, N), h_im + h_re)
        resid[1] = whole[1] - (resid[1] + dot3((ah[0], al[0]), imag))
        for half in range(2):
            rows = slice(half * 256, half * 256 + 256)
            re = resid[0, rows] + dot3((ah[1, rows], al[1, rows]), imag)
            im = resid[1, rows]
            resid[0, rows] = re
            put_rows(4, rows, re + im)
            put_rows(5, rows, re)
            put_rows(6, rows, im)
        sums = []
        for half in range(2):
            rows = slice(half * 256, half * 256 + 256)
            third = dot3(get(6, rows), get(7))
            second = dot3(get(5, rows), get(3))
            first = dot3(get(4, rows), get(2))
            re = first - third
            im = first + second
            pred[0, rows] = re
            pred[1, rows] = im
            numer = jnp.sum(resid[0, rows] * re + resid[1, rows] * im, axis=0, keepdims=True)
            denom = jnp.sum(re * re + im * im, axis=0, keepdims=True)
            sums.append((numer, denom))
        fold = []
        for value in (sums[0][0] + sums[1][0], sums[0][1] + sums[1][1]):
            value = value[:, :128] + value[:, 128:256] + value[:, 256:384] + value[:, 384:]
            fold.append(value + pltpu.roll(value, 64, 1))
        weight = freq_ref[me * 2 + j].astype(F32) * (1.0 / 512)
        total += weight * jnp.where(lanes < 64, fold[0], fold[1])
        if j == 0:
            for copy in out_copies(resid_out, pred_out, resid, pred, out_sem, 0):
                copy.start()

    stat[0] = total
    slots[me] = total
    for to in everyone:
        pltpu.make_async_remote_copy(
            src_ref=stat.at[0],
            dst_ref=slots.at[me],
            send_sem=stat_send,
            recv_sem=stat_recv,
            device_id=to,
            device_id_type=MESH,
        ).start()
    for copy in out_copies(resid_out, pred_out, resid, pred, out_sem, 1):
        copy.start()
    done = pltpu.make_async_remote_copy(
        src_ref=slots.at[pl.ds(0, 127)],
        dst_ref=slots.at[pl.ds(0, 127)],
        send_sem=stat_send,
        recv_sem=stat_recv,
        device_id=everyone[0],
        device_id_type=MESH,
    )
    for j in range(2):
        for h in range(2):
            arrival(j, h, 0, 127).wait_send()
    done.wait_recv()
    every = jnp.sum(slots[...], axis=0)
    numer = jnp.sum(jnp.where(lanes < 64, every, 0.0), axis=1, keepdims=True)
    denom = jnp.sum(jnp.where(lanes < 64, 0.0, every), axis=1, keepdims=True)
    step_out[...] = jnp.broadcast_to(numer / denom, (8, N))
    done.wait_send()
    for copy in out_copies(resid_out, pred_out, resid, pred, out_sem, 1):
        copy.wait()


def out_copies(resid_out, pred_out, resid, pred, sem, j):
    return (
        pltpu.make_async_copy(resid, resid_out.at[j], sem.at[j, 0]),
        pltpu.make_async_copy(pred, pred_out.at[j], sem.at[j, 1]),
    )


def final_kernel(resid, pred, step, resid_out, next_out, new, resid_sem, next_sem):
    copies = []
    for j in range(2):
        for c in range(2):
            copies.append(pltpu.make_async_copy(resid.at[j, c], resid_out.at[j, c], resid_sem.at[j * 2 + c]))
            copies[-1].start()
            for half in range(2):
                rows = slice(half * 256, half * 256 + 256)
                value = resid[j, c, rows, :] - jnp.tile(step[...], (32, 1)) * pred[j, c, rows, :]
                new[j, c, rows, :] = value
                at = (j, c, pl.ds(half * 256, 256))
                copies.append(pltpu.make_async_copy(new.at[at], next_out.at[at], next_sem.at[j * 4 + c * 2 + half]))
                copies[-1].start()
    for copy in copies:
        copy.wait()


def on_device(traces, freq_index, primaries):
    samples = traces.shape[2]
    anywhere, vmem = pl.BlockSpec(memory_space=pl.ANY), pl.BlockSpec(memory_space=pltpu.VMEM)
    big = jax.ShapeDtypeStruct((2, 2, N, N), F32)
    dma = pltpu.SemaphoreType.DMA
    resid, pred, step = pl.pallas_call(
        kernel,
        out_shape=(big, big, jax.ShapeDtypeStruct((8, N), F32)),
        in_specs=[pl.BlockSpec(memory_space=pltpu.HBM), anywhere, anywhere],
        out_specs=(anywhere, anywhere, vmem),
        scratch_shapes=[
            pltpu.VMEM((16, 4, 32, 1024), F32),
            pltpu.VMEM((2048, 1024), BF16),
            pltpu.VMEM((2048, 1024), BF16),
            pltpu.VMEM((2, 256, 1024), BF16),
            pltpu.VMEM((2, 256, 1024), BF16),
            pltpu.VMEM((4 * DEVICES * 16, 128), F32),
            pltpu.VMEM((4 * DEVICES * 16, 128), F32),
            pltpu.VMEM((2, N, N), F32),
            pltpu.VMEM((2, N, N), BF16),
            pltpu.VMEM((2, N, N), BF16),
            pltpu.VMEM((2, N, N), F32),
            pltpu.VMEM((2, N, N), F32),
            pltpu.SMEM((256,), jnp.int32),
            pltpu.VMEM((128, 128), jnp.int32),
            pltpu.VMEM((1, 1, 128), F32),
            pltpu.VMEM((DEVICES, 1, 128), F32),
            dma, dma((4,)), dma((4,)), dma((4,)), dma((32,)), dma((4,)), dma((2, 2)), dma, dma,
        ],
        compiler_params=pltpu.CompilerParams(
            collective_id=0, has_side_effects=True, vmem_limit_bytes=44 * 2**20
        ),
    )(pltpu.with_memory_space_constraint(freq_index, pltpu.HBM), traces.reshape(4, 16, 32, samples), primaries.reshape(2, 2, 4, 4, 32, N))
    return pl.pallas_call(
        final_kernel,
        out_shape=(big, big),
        in_specs=[vmem, vmem, vmem],
        out_specs=(anywhere, anywhere),
        scratch_shapes=[pltpu.VMEM((2, 2, N, N), F32), dma((4,)), dma((8,))],
        compiler_params=pltpu.CompilerParams(vmem_limit_bytes=16 * 2**20),
    )(resid, pred, step)


def solution(mesh):
    spec = P(("src", "rcv"), None, None, None)
    return jax.shard_map(
        on_device, mesh=mesh, in_specs=(P("src", "rcv", None), P(), spec), out_specs=(spec, spec), check_vma=False
    )
```

```python
import math
import random

import jax
import jax.numpy as jnp
from jax import lax
from jax.experimental import pallas as pl
from jax.experimental.pallas import tpu as pltpu
from jax.sharding import PartitionSpec as P

MESH = pl.DeviceIdType.MESH
F32, BF16 = jnp.float32, jnp.bfloat16
NN = (((1,), (0,)), ((), ()))
NT = (((1,), (1,)), ((), ()))
N = 512
DEVICES = 128


def far(x, y, z=0, h=0, c=0):
    return min(x, 4 - x) + min(y, 4 - y) + (0, 2, 1, 1)[2 * z + h]


def far_first():
    every = [(x, y, z, h, c) for x in range(4) for y in range(4) for z in range(2) for h in range(2) for c in range(2)]
    every = every[1:]
    random.Random(1).shuffle(every)
    return sorted(every, key=lambda offset: -far(*offset))


def relative_groups():
    every = [(x, y, z) for x in range(4) for y in range(4) for z in range(2)]
    random.Random(0).shuffle(every)
    return [every[i : i + 4] for i in range(0, 32, 4)]


def bunch_of(bunches, group):
    return [group in bunch for bunch in bunches].index(True)


def halves(x):
    high = x.astype(BF16)
    return high, (x - high.astype(F32)).astype(BF16)


def dot3(left, right, dims=NN):
    def one(a, b):
        return lax.dot_general(a, b, dims, preferred_element_type=F32)

    return one(left[0], right[0]) + (one(left[0], right[1]) + one(left[1], right[0]))


def cos_sin(steps):
    quarter = (steps + 128) >> 8
    angle = (steps - quarter * 256).astype(F32) * (2.0 * math.pi / 1024)
    square = angle * angle
    cos = 1.0 / 40320 - square * (1.0 / 3628800)
    for term in (-1.0 / 720, 1.0 / 24, -0.5, 1.0):
        cos = term + square * cos
    sin = -1.0 / 5040 + square * (1.0 / 362880)
    for term in (1.0 / 120, -1.0 / 6, 1.0):
        sin = term + square * sin
    sin = angle * sin
    quarter = quarter & 3
    odd = (quarter & 1) == 1
    cos, sin = jnp.where(odd, sin, cos), jnp.where(odd, cos, sin)
    cos = jnp.where((quarter == 1) | (quarter == 2), -cos, cos)
    sin = jnp.where(quarter >= 2, -sin, sin)
    return cos, sin


def kernel(
    freq_hbm, traces_ref, prim_ref,
    resid_out, pred_out, step_out,
    raw, xh, xl, th, tl, sbuf, rbuf, whole, ah, al, resid, pred, freq_ref, freqs, stat, slots,
    freq_sem, raw_sem, prim_sem, send_sem, recv_sem, own_sem, out_sem, stat_send, stat_recv,
):
    src, rcv = lax.axis_index("src"), lax.axis_index("rcv")
    me = src * 16 + rcv
    xs = [(rcv // 4 + d) % 4 for d in range(4)]
    ys = [(src // 2 + d) % 4 for d in range(4)]
    z_low = [(src + d) % 2 for d in range(2)]
    z_high = [(rcv // 2 + d) % 2 for d in range(2)]
    cores = [(rcv + d) % 2 for d in range(2)]
    groups = relative_groups()

    offsets = far_first()
    order = [offset for bunch in groups for group in bunch for offset in sorted(offsets) if offset[:3] == group]

    def target(offset):
        x, y, z, h, c = offset
        return ys[y] * 2 + z_low[z], xs[x] * 4 + z_high[h] * 2 + cores[c]

    everyone = [target(offset) for offset in offsets]
    home = bunch_of(groups, (0, 0, 0))

    def load(b, g):
        rows = pl.ds(b * 4, 4)
        return pltpu.make_async_copy(traces_ref.at[g, rows], raw.at[rows, g], raw_sem.at[b])

    freq_copy = pltpu.make_async_copy(freq_hbm, freq_ref, freq_sem)
    freq_copy.start()
    for b in range(4):
        for g in range(4):
            load(b, g).start()

    barrier = pltpu.get_barrier_semaphore()
    for to in everyone:
        pl.semaphore_signal(barrier, inc=1, device_id=to, device_id_type=MESH)

    lane = lax.broadcasted_iota(jnp.int32, (128, 128), 1)

    def table(j):
        for d in range(128):
            freqs[d : d + 1, :] = jnp.full((1, 128), freq_ref[2 * d + j], jnp.int32)
        freq = freqs[...]
        cos, sin = cos_sin((freq * lane) & 1023)
        cos, sin = cos * 0.03125, sin * 0.03125
        turn_cos, turn_sin = cos_sin((freq * 128) & 1023)
        sign = 1.0 - 2.0 * (freq & 1).astype(F32)
        for a in range(4):
            if a:
                cos, sin = cos * turn_cos - sin * turn_sin, sin * turn_cos + cos * turn_sin
            for c, part in enumerate((cos, -sin)):
                for k, value in ((a, part), (a + 4, part * sign)):
                    high, low = halves(value)
                    th[j, c * 128 : c * 128 + 128, k * 128 : k * 128 + 128] = high
                    tl[j, c * 128 : c * 128 + 128, k * 128 : k * 128 + 128] = low

    def transform(h, b):
        rows = slice((h * 2 + b) * 512, (h * 2 + b) * 512 + 512)
        out = dot3((th[0], tl[0]), (xh[rows, :], xl[rows, :]), NT)
        for c in range(2):
            for d in range(0, 128, 8):
                for i in range(4):
                    start = (h * DEVICES + d) * 16 + c * 8 + b * 4 + i
                    sbuf[pl.ds(start, 8, stride=16), :] = out[
                        c * 128 + d : c * 128 + d + 8, i * 128 : i * 128 + 128
                    ]

    def transform_part(c):
        @pl.loop(0, 4)
        def _(b):
            rows = pl.ds(pl.multiple_of(b * 512, 512), 512)
            part = slice(c * 128, c * 128 + 128)
            out = dot3((th[1, part], tl[1, part]), (xh[rows, :], xl[rows, :]), NT)
            for d in range(0, 128, 8):
                for i in range(4):
                    start = ((2 + c) * DEVICES + d) * 16 + b * 4 + i
                    sbuf[pl.ds(start, 8, stride=16), :] = out[d : d + 8, i * 128 : i * 128 + 128]

    def piece(j, h, index, count=1):
        return pl.ds(pl.multiple_of(((j * 2 + h) * DEVICES + index) * 16, 16), 16 * count)

    def own(j, h):
        return pltpu.make_async_copy(sbuf.at[piece(j, h, me)], rbuf.at[piece(j, h, me)], own_sem.at[j * 2 + h])

    def send(j, h):
        own(j, h).start()
        for offset in order:
            to, k = target(offset), bunch_of(groups, offset[:3])
            pltpu.make_async_remote_copy(
                src_ref=sbuf.at[piece(j, h, to[0] * 16 + to[1])],
                dst_ref=rbuf.at[piece(j, h, me)],
                send_sem=send_sem.at[j * 2 + h],
                recv_sem=recv_sem.at[(j * 2 + h) * 8 + k],
                device_id=to,
                device_id_type=MESH,
            ).start()

    def arrival(j, h, k, count):
        return pltpu.make_async_remote_copy(
            src_ref=sbuf.at[piece(j, h, 0, count)],
            dst_ref=rbuf.at[piece(j, h, 0, count)],
            send_sem=send_sem.at[j * 2 + h],
            recv_sem=recv_sem.at[(j * 2 + h) * 8 + k],
            device_id=everyone[0],
            device_id_type=MESH,
        )

    freq_copy.wait()
    table(0)
    for h in range(2):
        for b in range(2):
            n = h * 2 + b
            for g in range(4):
                load(n, g).wait()
            high, low = halves(raw[n * 4 : n * 4 + 4].reshape(512, 1024))
            xh[n * 512 : n * 512 + 512, :] = high
            xl[n * 512 : n * 512 + 512, :] = low
            transform(h, b)
        if h == 0:
            pl.semaphore_wait(barrier, DEVICES - 1)
        send(0, h)

    def prim_copy(j, c):
        return pltpu.make_async_copy(
            prim_ref.at[j, c], raw.at[pl.ds(4 * c, 4), :, :, pl.ds(j * N, N)], prim_sem.at[j * 2 + c]
        )

    for j in range(2):
        for c in range(2):
            prim_copy(j, c).start()

    table(1)
    for c in range(2):
        transform_part(c)
        send(1, c)

    wide = lax.broadcasted_iota(jnp.int32, (16, 128), 1)
    odd, upper = (wide // 32) % 2 == 1, wide >= 64
    lanes = lax.broadcasted_iota(jnp.int32, (1, 128), 1)
    total = jnp.zeros((1, 128), F32)

    def place(slot, rows=slice(0, N)):
        base = slot % 4 * N
        return slice(base + rows.start, base + rows.stop), slice(slot // 4 * N, slot // 4 * N + N)

    def put_rows(slot, rows, value):
        at = place(slot, rows)
        xh[at], xl[at] = halves(value)

    def get(slot, rows=slice(0, N)):
        at = place(slot, rows)
        return xh[at], xl[at]

    def model_operands(j):
        for c in range(2):
            prim_copy(j, c).wait()
        model = [raw[4 * c : 4 * c + 4, :, :, j * N : j * N + N].reshape(N, N) for c in range(2)]
        for index, value in enumerate(model):
            ah[index], al[index] = halves(value)

    def assemble(j, h, store):
        for k, bunch in enumerate(groups):
            if k == home:
                own(j, h).wait()
            arrival(j, h, k, 15 if k == home else 16).wait_recv()
            for x, y, z in bunch:
                from_x, from_s = xs[-x % 4], ys[-y % 4] * 2 + z_low[z]
                v = [rbuf[piece(j, h, from_s * 16 + from_x * 4 + q), :] for q in range(4)]
                for m in (0, 2):
                    a, b = v[m], v[m + 1]
                    v[m] = jnp.where(odd, pltpu.roll(b, 32, 1), a)
                    v[m + 1] = jnp.where(odd, b, pltpu.roll(a, 96, 1))
                for m in (0, 1):
                    a, b = v[m], v[m + 2]
                    v[m] = jnp.where(upper, pltpu.roll(b, 64, 1), a)
                    v[m + 2] = jnp.where(upper, b, pltpu.roll(a, 64, 1))
                columns = pl.ds(pl.multiple_of(from_x * 128, 128), 128)
                for g in range(4):
                    store(h, from_s * 64 + g * 16, columns, v[g])

    def store_both(h, row, columns, value):
        rows = pl.ds(pl.multiple_of(row + h * 8, 8), 8)
        whole[0, rows, columns] = value[:8]
        whole[1, rows, columns] = value[8:]

    def store_part(c, row, columns, value):
        whole[c, pl.ds(pl.multiple_of(row, 16), 16), columns] = value

    def symmetric(c, then):
        for p in range(4):
            for q in range(p, 4):
                a, b = slice(p * 128, p * 128 + 128), slice(q * 128, q * 128 + 128)
                first, second = whole[c, a, b], whole[c, b, a]
                value = 0.5 * (first + second.T)
                whole[c, a, b] = value
                then(a, b, value)
                if p != q:
                    value = 0.5 * (second + first.T)
                    whole[c, b, a] = value
                    then(b, a, value)

    def put_block(slot, rows, columns, value):
        high, low = halves(value)
        at = slice(slot * N + rows.start, slot * N + rows.stop)
        xh[at, columns] = high
        xl[at, columns] = low

    def real_operands(rows, columns, value):
        put_block(0, rows, columns, value)

    def imag_operands(rows, columns, value):
        put_block(1, rows, columns, value)

    def gram(matrix):
        high, low = matrix
        square = lax.dot_general(high, high, NN, preferred_element_type=F32)
        mixed = lax.dot_general(high, low, NN, preferred_element_type=F32)
        return square + (mixed + mixed.T)

    def real_products():
        real = get(0)
        resid[0] = whole[0] - dot3((ah[0], al[0]), real)
        resid[1] = dot3((ah[1], al[1]), real)
        pred[0] = gram(real)

    for j in range(2):
        model_operands(j)
        if j == 0:

            @pl.loop(0, 2)
            def _(h):
                assemble(0, h, store_both)

            symmetric(0, real_operands)
            real_products()
        else:
            assemble(1, 0, store_part)
            symmetric(0, real_operands)
            for copy in out_copies(resid_out, pred_out, resid, pred, out_sem, 0):
                copy.wait()
            real_products()
            assemble(1, 1, store_part)
        symmetric(1, imag_operands)

        imag = get(1)
        cross = dot3(get(0), imag)
        h_re = pred[0] + gram(imag)
        h_im = cross - cross.T
        put_rows(2, slice(0, N), h_re)
        put_rows(3, slice(0, N), h_im - h_re)
        put_rows(7, slice(0, N), h_im + h_re)
        resid[1] = whole[1] - (resid[1] + dot3((ah[0], al[0]), imag))
        for half in range(2):
            rows = slice(half * 256, half * 256 + 256)
            re = resid[0, rows] + dot3((ah[1, rows], al[1, rows]), imag)
            im = resid[1, rows]
            resid[0, rows] = re
            put_rows(4, rows, re + im)
            put_rows(5, rows, re)
            put_rows(6, rows, im)
        sums = []
        for half in range(2):
            rows = slice(half * 256, half * 256 + 256)
            third = dot3(get(6, rows), get(7))
            second = dot3(get(5, rows), get(3))
            first = dot3(get(4, rows), get(2))
            re = first - third
            im = first + second
            pred[0, rows] = re
            pred[1, rows] = im
            numer = jnp.sum(resid[0, rows] * re + resid[1, rows] * im, axis=0, keepdims=True)
            denom = jnp.sum(re * re + im * im, axis=0, keepdims=True)
            sums.append((numer, denom))
        fold = []
        for value in (sums[0][0] + sums[1][0], sums[0][1] + sums[1][1]):
            value = value[:, :128] + value[:, 128:256] + value[:, 256:384] + value[:, 384:]
            fold.append(value + pltpu.roll(value, 64, 1))
        weight = freq_ref[me * 2 + j].astype(F32) * (1.0 / 512)
        total += weight * jnp.where(lanes < 64, fold[0], fold[1])
        if j == 0:
            for copy in out_copies(resid_out, pred_out, resid, pred, out_sem, 0):
                copy.start()

    stat[0] = total
    slots[me] = total
    for to in everyone:
        pltpu.make_async_remote_copy(
            src_ref=stat.at[0],
            dst_ref=slots.at[me],
            send_sem=stat_send,
            recv_sem=stat_recv,
            device_id=to,
            device_id_type=MESH,
        ).start()
    for copy in out_copies(resid_out, pred_out, resid, pred, out_sem, 1):
        copy.start()
    done = pltpu.make_async_remote_copy(
        src_ref=slots.at[pl.ds(0, 127)],
        dst_ref=slots.at[pl.ds(0, 127)],
        send_sem=stat_send,
        recv_sem=stat_recv,
        device_id=everyone[0],
        device_id_type=MESH,
    )
    for j in range(2):
        for h in range(2):
            arrival(j, h, 0, 127).wait_send()
    done.wait_recv()
    every = jnp.sum(slots[...], axis=0)
    numer = jnp.sum(jnp.where(lanes < 64, every, 0.0), axis=1, keepdims=True)
    denom = jnp.sum(jnp.where(lanes < 64, 0.0, every), axis=1, keepdims=True)
    step_out[...] = jnp.broadcast_to(numer / denom, (8, N))
    done.wait_send()
    for copy in out_copies(resid_out, pred_out, resid, pred, out_sem, 1):
        copy.wait()


def out_copies(resid_out, pred_out, resid, pred, sem, j):
    return (
        pltpu.make_async_copy(resid, resid_out.at[j], sem.at[j, 0]),
        pltpu.make_async_copy(pred, pred_out.at[j], sem.at[j, 1]),
    )


def final_kernel(resid, pred, step, resid_out, next_out, new, resid_sem, next_sem):
    places = [(j, c) for j in range(2) for c in range(2)]
    copies = [pltpu.make_async_copy(resid.at[at], resid_out.at[at], resid_sem.at[n]) for n, at in enumerate(places)]
    for copy in copies:
        copy.start()
    for n, (j, c) in enumerate(places):
        for half in range(2):
            rows = slice(half * 256, half * 256 + 256)
            new[j, c, rows, :] = resid[j, c, rows, :] - jnp.tile(step[...], (32, 1)) * pred[j, c, rows, :]
            at = (j, c, pl.ds(half * 256, 256))
            copies.append(pltpu.make_async_copy(new.at[at], next_out.at[at], next_sem.at[n * 2 + half]))
            copies[-1].start()
    for copy in copies:
        copy.wait()


def on_device(traces, freq_index, primaries):
    samples = traces.shape[2]
    anywhere, vmem = pl.BlockSpec(memory_space=pl.ANY), pl.BlockSpec(memory_space=pltpu.VMEM)
    big = jax.ShapeDtypeStruct((2, 2, N, N), F32)
    dma = pltpu.SemaphoreType.DMA
    resid, pred, step = pl.pallas_call(
        kernel,
        out_shape=(big, big, jax.ShapeDtypeStruct((8, N), F32)),
        in_specs=[pl.BlockSpec(memory_space=pltpu.HBM), anywhere, anywhere],
        out_specs=(anywhere, anywhere, vmem),
        scratch_shapes=[
            pltpu.VMEM((16, 4, 32, 1024), F32),
            pltpu.VMEM((2048, 1024), BF16),
            pltpu.VMEM((2048, 1024), BF16),
            pltpu.VMEM((2, 256, 1024), BF16),
            pltpu.VMEM((2, 256, 1024), BF16),
            pltpu.VMEM((4 * DEVICES * 16, 128), F32),
            pltpu.VMEM((4 * DEVICES * 16, 128), F32),
            pltpu.VMEM((2, N, N), F32),
            pltpu.VMEM((2, N, N), BF16),
            pltpu.VMEM((2, N, N), BF16),
            pltpu.VMEM((2, N, N), F32),
            pltpu.VMEM((2, N, N), F32),
            pltpu.SMEM((256,), jnp.int32),
            pltpu.VMEM((128, 128), jnp.int32),
            pltpu.VMEM((1, 1, 128), F32),
            pltpu.VMEM((DEVICES, 1, 128), F32),
            dma, dma((4,)), dma((4,)), dma((4,)), dma((32,)), dma((4,)), dma((2, 2)), dma, dma,
        ],
        compiler_params=pltpu.CompilerParams(
            collective_id=0, has_side_effects=True, vmem_limit_bytes=44 * 2**20
        ),
    )(pltpu.with_memory_space_constraint(freq_index, pltpu.HBM), traces.reshape(4, 16, 32, samples), primaries.reshape(2, 2, 4, 4, 32, N))
    return pl.pallas_call(
        final_kernel,
        out_shape=(big, big),
        in_specs=[vmem, vmem, vmem],
        out_specs=(anywhere, anywhere),
        scratch_shapes=[pltpu.VMEM((2, 2, N, N), F32), dma((4,)), dma((8,))],
        compiler_params=pltpu.CompilerParams(vmem_limit_bytes=16 * 2**20),
    )(resid, pred, step)


def solution(mesh):
    spec = P(("src", "rcv"), None, None, None)
    return jax.shard_map(
        on_device, mesh=mesh, in_specs=(P("src", "rcv", None), P(), spec), out_specs=(spec, spec), check_vma=False
    )
```
